32 devices in a mesh: region: 16 (over z, y, core), coord: 2 (over x).
Axes of the slice: x: 2, y: 2, z: 4, core: 2. Of those that a mesh axis runs over, the one named last changes fastest.
Arguments:
- right_side: float32 [2, 65536], P(None, ('region', 'coord')), may hold values from -6 to 6
- anchor: float32 [65536], P(('region', 'coord')), may hold values from 0.5 to 2
- blocks: float32 [512, 2, 128, 128], P(('region', 'coord')), may hold values from 2.734375e-05 to 0.02734375
- tile_nbr: int32 [512, 2], P(('region', 'coord')), may hold values from 0 to 31
- cut_cells: int32 [32, 32, 128], P(('region', 'coord')), may hold values from 0 to 2047
- cut_weight: float32 [32, 32, 128], P(('region', 'coord')), may hold values from 0 to 1, as said below
- pin_cell: int32 [131072], P(('region', 'coord')), may hold values from 0 to 2047
- pin_net: int32 [131072], P(('region', 'coord')), may hold values from 0 to 4095, as said below
- star_weight: float32 [4096], replicated, may hold values from 0.2 to 2
Outputs:
- positions: float32 [2, 65536], P(None, ('region', 'coord'))
- residual: float32 [2, 65536], P(None, ('region', 'coord'))
The draws below stay inside these ranges and needn't reach their ends.
Inputs may be any that keep to these rules, and one draw needn't show every extreme that they name: cut_weight[d, p, s] equals cut_weight[p, d, s], and it is 0 where p equals d. Every net number appears exactly 32 times; net n is owned by partition n // 128, and pin_net[d * 4096 + o * 128 + s] is a net owned by partition o for every partition d, owner o and s below 128.
All inputs are finite; a program needn't handle non-finite values.
Results may differ from the reference program's by a relative error of at most 0.00021.
Values sent between devices are 32-bit elements; how exact they have to be, the bound alone decides.
A program may use at most 128 MiB of HBM per device.

```python
import math
import jax
import jax.numpy as jnp
from jax import lax

TILE = 128
TILES = 16
NB = 2
CUT = 128
NETS_DEV = 128
FANOUT = 32
ITERS = 3
PARTITIONS = 32
TILES_ALL = 512
CELLS = 65536
NETS = 4096
PINS_DEV = 4096
PINS = 131072
N_REGION = 16
N_COORD = 2


def draw_right_side(key, part):
    region = jnp.arange(CELLS, dtype=jnp.int32) // (TILES * TILE)
    fraction = region.astype(jnp.float32) / max(PARTITIONS - 1, 1)
    spread = 0.6 * jnp.exp(fraction * jnp.log(3.0))
    values = jax.random.normal(key, (2, CELLS)) * spread
    return jnp.clip(values, -6.0, 6.0)


def draw_cut_weight(key, part):
    dims = (PARTITIONS, PARTITIONS, CUT)
    drawn = jnp.exp(jax.random.uniform(key, dims, minval=jnp.log(0.1), maxval=0.0))
    blended = 0.5 * (drawn + jnp.swapaxes(drawn, 0, 1))
    diagonal_pair = jnp.arange(PARTITIONS)[:, None] == jnp.arange(PARTITIONS)[None, :]
    return jnp.where(diagonal_pair[:, :, None], 0.0, blended)


def draw_pin_net(key, part):
    per_owner = NETS_DEV * FANOUT
    slot_count = per_owner // PARTITIONS
    labels = jnp.arange(per_owner, dtype=jnp.int32) // FANOUT
    owner_keys = jax.random.split(key, PARTITIONS)
    shuffled = jax.vmap(lambda owner_key: jax.random.permutation(owner_key, labels))(owner_keys)
    nets = shuffled + (jnp.arange(PARTITIONS, dtype=jnp.int32) * NETS_DEV)[:, None]
    blocked = nets.reshape(PARTITIONS, PARTITIONS, slot_count)
    return jnp.transpose(blocked, (1, 0, 2)).reshape(-1)


def plant(result, stream_key, smallest, top_value):
    place = [jax.random.randint(jax.random.fold_in(stream_key, axis), (), 0, length) for axis, length in enumerate(result.shape)]
    longest = result.shape.index(max(result.shape))
    next_to = place[:longest] + [(place[longest] + 1) % result.shape[longest]] + place[longest + 1:]
    return result.at[tuple(place)].set(smallest).at[tuple(next_to)].set(top_value)


def block_levels(rng, extent, pieces, smallest, top_value):
    def one(dim, shards_of):
        heights = jax.random.uniform(jax.random.fold_in(jax.random.fold_in(rng, 6), dim), (shards_of,), jnp.float32, smallest / len(pieces), top_value / len(pieces))
        return jnp.repeat(jnp.exp(heights), extent[dim] // shards_of).reshape((-1,) + (1,) * (len(extent) - dim - 1))

    loudness = one(*pieces[0])
    for cut in pieces[1:]:
        loudness = loudness * one(*cut)
    return loudness


def setup_inputs(seed: int = 0) -> dict:
    arg_keys = jax.random.split(jax.random.key(seed), 10)
    return {
        "right_side": draw_right_side(jax.random.fold_in(arg_keys[9], 71), 0),
        "anchor": jnp.clip(0.5 + 1.5 * jax.random.uniform(arg_keys[1], (CELLS,), jnp.float32) ** block_levels(arg_keys[1], (CELLS,), ((0, 32),), -0.2, 0.2), 0.5, 2.0),
        "blocks": jnp.clip(jnp.exp(math.log(0.02734375) - 6.9077552 * jax.random.uniform(arg_keys[2], (TILES_ALL, NB, TILE, TILE), jnp.float32) ** block_levels(arg_keys[2], (TILES_ALL, NB, TILE, TILE), ((0, 32),), -0.2, 0.2)), 2.7343750844011083e-05, 0.02734375),
        "tile_nbr": plant(jax.random.randint(arg_keys[3], (TILES_ALL, NB), 0, N_COORD * TILES), jax.random.fold_in(arg_keys[3], 1), 0, (N_COORD * TILES) - 1).astype(jnp.int32),
        "cut_cells": plant(jax.random.randint(arg_keys[4], (PARTITIONS, PARTITIONS, CUT), 0, TILES * TILE), jax.random.fold_in(arg_keys[4], 1), 0, (TILES * TILE) - 1).astype(jnp.int32),
        "cut_weight": draw_cut_weight(jax.random.fold_in(arg_keys[9], 71), 0),
        "pin_cell": plant(jax.random.randint(arg_keys[6], (PINS,), 0, TILES * TILE), jax.random.fold_in(arg_keys[6], 1), 0, (TILES * TILE) - 1).astype(jnp.int32),
        "pin_net": draw_pin_net(jax.random.fold_in(arg_keys[9], 71), 0),
        "star_weight": jnp.clip(jnp.exp(jax.random.uniform(arg_keys[8], (NETS,), jnp.float32, math.log(0.2), math.log(2.0))), 0.2, 2.0),
    }


exact_prec = lax.Precision.HIGHEST


def region_apply(inputs):
    region_blocks, neighbours, vectors = inputs
    forward = jnp.einsum("tkij,ctkj->cti", region_blocks, vectors[:, neighbours], precision=exact_prec)
    backward = jnp.einsum("tkij,cti->ctkj", region_blocks, vectors, precision=exact_prec)
    flat_back = backward.reshape(vectors.shape[0], -1, vectors.shape[2])
    spread = jnp.zeros_like(vectors).at[:, neighbours.reshape(-1)].add(flat_back)
    return forward + spread


def region_degree(inputs):
    region_blocks, neighbours = inputs
    row_sums = jnp.sum(region_blocks, axis=(1, 3))
    col_sums = jnp.sum(region_blocks, axis=2).reshape(-1, region_blocks.shape[3])
    return row_sums + jnp.zeros_like(row_sums).at[neighbours.reshape(-1)].add(col_sums)


def reference(right_side, anchor, blocks, tile_nbr, cut_cells, cut_weight, pin_cell, pin_net, star_weight):
    region_tiles = N_COORD * TILES
    cells_dev = TILES * TILE
    region_blocks = blocks.reshape(N_REGION, region_tiles, NB, TILE, TILE)
    neighbours = tile_nbr.reshape(N_REGION, region_tiles, NB)
    degree = lax.map(region_degree, (region_blocks, neighbours)).reshape(-1)
    offsets = jnp.arange(PARTITIONS, dtype=jnp.int32) * cells_dev
    own_cells = (cut_cells + offsets[:, None, None]).reshape(-1)
    peer_cells = (jnp.swapaxes(cut_cells, 0, 1) + offsets[None, :, None]).reshape(-1)
    link_weights = cut_weight.reshape(-1)
    pin_owner = jnp.arange(PINS, dtype=jnp.int32) // PINS_DEV
    pin_global = pin_cell + pin_owner * cells_dev
    pin_weight = star_weight[pin_net]
    degree = degree + jnp.zeros((CELLS,), jnp.float32).at[own_cells].add(link_weights)
    degree = degree + jnp.zeros((CELLS,), jnp.float32).at[pin_global].add(pin_weight)
    degree = degree + anchor

    def operate(vectors):
        by_region = jnp.transpose(vectors.reshape(2, N_REGION, region_tiles, TILE), (1, 0, 2, 3))
        local_part = lax.map(region_apply, (region_blocks, neighbours, by_region))
        local_part = jnp.transpose(local_part, (1, 0, 2, 3)).reshape(2, CELLS)
        cut_part = jnp.zeros((2, CELLS), jnp.float32).at[:, own_cells].add(link_weights * vectors[:, peer_cells])
        totals = jnp.zeros((2, NETS), jnp.float32).at[:, pin_net].add(vectors[:, pin_global])
        centre = totals / FANOUT
        star_part = jnp.zeros((2, CELLS), jnp.float32).at[:, pin_global].add(pin_weight * centre[:, pin_net])
        return degree * vectors - local_part - cut_part - star_part

    positions = jnp.zeros_like(right_side)
    residual = right_side
    direction = right_side
    norm_now = jnp.sum(residual * residual, axis=1, keepdims=True)
    for iteration in range(ITERS):
        applied = operate(direction)
        step_size = norm_now / jnp.sum(direction * applied, axis=1, keepdims=True)
        positions = positions + step_size * direction
        residual = residual - step_size * applied
        norm_next = jnp.sum(residual * residual, axis=1, keepdims=True)
        direction = residual + (norm_next / norm_now) * direction
        norm_now = norm_next
    return positions, residual
```

```python
import functools

import jax
import jax.numpy as jnp
from jax import lax
from jax.experimental import pallas as pl
from jax.experimental.pallas import tpu as pltpu
from jax.sharding import PartitionSpec as P

FANOUT = 32
ITERS = 3
LANES = 128
GROUP = 4
MESH = pl.DeviceIdType.MESH
F32 = jnp.float32
BF16 = jnp.bfloat16

NN = (((1,), (0,)), ((), ()))
NT = (((1,), (1,)), ((), ()))


def mm(a, b, dims=NN):
    return lax.dot_general(a, b, dims, preferred_element_type=F32)


def pieces(x):
    high = x.astype(BF16)
    low = (x - high.astype(F32)).astype(BF16)
    return high, low


def kernel(
    regions,
    halves,
    rs_hbm,
    anchor_hbm,
    blocks_ref,
    nbr_row_hbm,
    cut_cell_hbm,
    cut_w_hbm,
    pin_cell_hbm,
    pin_net_hbm,
    star_w_hbm,
    out_ref,
    rs_ref,
    anchor_ref,
    nbr_row_ref,
    cut_cell_ref,
    cut_w_ref,
    pin_cell_ref,
    pin_net_ref,
    star_w_ref,
    onehot,
    himask,
    block_buf,
    nethot,
    quad,
    lhs_b,
    lhs_f,
    back,
    front,
    send_star,
    recv_star,
    send_cut,
    recv_cut,
    send2,
    recv2,
    dot_send,
    dot_recv,
    star_energy,
    vec_send,
    vec_recv,
    spr_send,
    spr_recv,
    sems,
    in_sems,
):
    count = regions * halves
    first_owner = regions // 4
    owner_regions = regions - 2 * first_owner
    owners = owner_regions * halves
    share = count // owners
    tiles = anchor_ref.shape[0]
    cut_groups = count // GROUP
    pin_chunks = pin_cell_ref.shape[0]
    pin_groups = pin_chunks // GROUP
    per_chunk = count // pin_chunks
    wide = GROUP * LANES
    my_region = lax.axis_index("region")
    my_half = lax.axis_index("coord")
    me = my_region * halves + my_half
    partner = (my_region, 1 - my_half)
    owning = jnp.logical_and(my_region >= first_owner, my_region < first_owner + owner_regions)
    my_share = (my_region - first_owner) * halves + my_half

    def each_other(act):
        act(my_region * halves + 1 - my_half, partner)

        @pl.loop(1, regions, unroll=True if regions <= 16 else 4)
        def _(step):
            region = my_region + step
            region = jnp.where(region >= regions, region - regions, region)
            for flip in range(halves):
                half = my_half if flip == 0 else 1 - my_half
                act(region * halves + half, (region, half))

    def each_owner(act):
        mine = lax.rem(my_region + owner_regions - first_owner % owner_regions, owner_regions)

        def at(step):
            place = mine + step
            return jnp.where(place >= owner_regions, place - owner_regions, place)

        @pl.loop(1, owner_regions, unroll=True if regions <= 16 else 4)
        def _(step):
            place = at(step)
            for flip in range(halves):
                half = my_half if flip == 0 else 1 - my_half
                act(place * halves + half, (place + first_owner, half))

        act(mine * halves + 1 - my_half, (mine + first_owner, 1 - my_half))

        @pl.when(jnp.logical_not(owning))
        def _():
            act(mine * halves + my_half, (mine + first_owner, my_half))

    def over_groups(groups, body):
        if groups <= 8:
            for group in range(groups):
                body(group)
        else:
            pl.loop(0, groups, unroll=4)(body)

    def sum_groups(groups, body, total):
        if groups <= 8:
            for group in range(groups):
                total = body(group, total)
            return total
        return lax.fori_loop(0, groups, body, total, unroll=4)

    barrier = pltpu.get_barrier_semaphore()

    def greet(other, device):
        pl.semaphore_signal(barrier, inc=1, device_id=device, device_id_type=MESH)

    each_other(greet)
    load = {}
    for k, (name, source, target) in enumerate(
        (
            ("pin_cell", pin_cell_hbm, pin_cell_ref),
            ("pin_net", pin_net_hbm, pin_net_ref),
            ("rs", rs_hbm, rs_ref),
            ("cut_cell", cut_cell_hbm, cut_cell_ref),
            ("nbr", nbr_row_hbm, nbr_row_ref),
            ("star_w", star_w_hbm, star_w_ref),
            ("cut_w", cut_w_hbm, cut_w_ref),
            ("anchor", anchor_hbm, anchor_ref),
            ("blocks", blocks_ref, block_buf),
        )
    ):
        load[name] = pltpu.make_async_copy(source, target, in_sems.at[k])
        load[name].start()
    star_energy[...] = jnp.zeros_like(star_energy)

    iota_lo = lax.broadcasted_iota(jnp.int32, (LANES, LANES), 0)
    iota_hi = lax.broadcasted_iota(jnp.int32, (tiles, LANES), 0)
    iota_net = lax.broadcasted_iota(jnp.int32, (per_chunk * LANES, LANES), 0)
    lane = lax.broadcasted_iota(jnp.int32, (1, LANES), 1)

    def put_onehot(group, place, cells):
        lanes = slice(place * LANES, (place + 1) * LANES)
        low = lax.bitwise_and(cells, LANES - 1)
        high = lax.shift_right_logical(cells, 7)
        onehot[group, :, lanes] = (iota_lo == low).astype(F32).astype(BF16)
        himask[group, :, lanes] = (iota_hi == high).astype(F32)

    def hot_pins(group):
        for place in range(GROUP):
            chunk = group * GROUP + place
            put_onehot(cut_groups + group, place, pin_cell_ref[pl.ds(chunk, 1), :])
            net = pin_net_ref[pl.ds(chunk, 1), :] - chunk * (per_chunk * LANES)
            nethot[chunk] = (iota_net == net).astype(F32).astype(BF16)

    def hot_cut(group):
        for place in range(GROUP):
            put_onehot(group, place, cut_cell_ref[pl.ds(group * GROUP + place, 1), :])

    load["pin_cell"].wait()
    load["pin_net"].wait()
    over_groups(pin_groups, hot_pins)

    def hold_blocks():
        load["blocks"].wait()

        @pl.loop(0, tiles, unroll=4)
        def _(tile):
            for k in range(2):
                high, low = pieces(block_buf[2 * tile + k])
                lanes = slice(k * LANES, (k + 1) * LANES)
                quad[tile, :LANES, lanes] = high
                quad[tile, LANES:, lanes] = low

        ones_row = jnp.where(lax.broadcasted_iota(jnp.int32, (8, 2 * LANES), 0) == 4, 1.0, 0.0)
        for tile in range(tiles):
            lhs_b[tile] = ones_row
            lhs_f[tile] = ones_row

    load["nbr"].wait()
    shift = my_half * tiles
    span = 2 * tiles
    rel_row = nbr_row_ref[...] - shift
    rel_row = jnp.where(rel_row < 0, rel_row + span, rel_row)
    on_diagonal = lax.broadcasted_iota(jnp.int32, (tiles, tiles), 0) == lax.broadcasted_iota(
        jnp.int32, (tiles, tiles), 1
    )
    rel_col = [
        jnp.sum(
            jnp.where(on_diagonal, rel_row[k : k + 1, :].astype(F32), 0.0), axis=1, keepdims=True
        ).astype(jnp.int32)
        for k in range(2)
    ]
    spread_hot = [
        (lax.broadcasted_iota(jnp.int32, (span, tiles), 0) == rel_row[k : k + 1, :])
        .astype(F32)
        .astype(BF16)
        for k in range(2)
    ]
    select_hot = [
        (lax.broadcasted_iota(jnp.int32, (tiles, span), 1) == rel_col[k])
        .astype(F32)
        .astype(BF16)
        for k in range(2)
    ]

    def rows8(first, second):
        fh, fl = pieces(first)
        sh, sl = pieces(second)
        stacked = jnp.concatenate(
            [x.astype(F32) for x in (fh, sh, fl, sl)]
            + [jnp.zeros((4, first.shape[1]), F32)],
            axis=0,
        )
        return stacked.astype(BF16)

    def gathered(group, left):
        got = mm(left, onehot[group])
        got = got[: 2 * tiles] + got[2 * tiles :]
        mask = himask[group]
        return [
            jnp.sum(got[c * tiles : (c + 1) * tiles] * mask, axis=0, keepdims=True)
            for c in range(2)
        ]

    def scattered(group, rows):
        mask = himask[group]
        spread = jnp.concatenate([mask * row for row in rows], axis=0)
        high, low = pieces(spread)
        both = mm(jnp.concatenate([high, low], axis=0), onehot[group], NT)
        rows_all = len(rows) * tiles
        return both[:rows_all] + both[rows_all:]

    def dot_rows(values):
        row = jnp.zeros((1, LANES), F32)
        for k, (a, b) in enumerate(values):
            total = jnp.sum(jnp.sum(a * b, axis=0, keepdims=True), axis=1, keepdims=True)
            row = jnp.where(lane == k, total, row)
        return row

    def halves_of(x):
        return x[:tiles], x[tiles:]

    def send_all(source_of, target, slot):
        def send(other, device):
            pltpu.make_async_remote_copy(
                src_ref=source_of(other),
                dst_ref=target.at[me],
                send_sem=sems.at[slot],
                recv_sem=sems.at[slot + 1],
                device_id=device,
                device_id_type=MESH,
            ).start()

        each_other(send)

    def wait_all(like, slot, messages=count - 1):
        part = like.at[pl.ds(0, messages)]
        pltpu.make_async_copy(part, part, sems.at[slot]).wait()

    def for_owner(act):
        pl.when(owning)(lambda: act(owners - 1))
        pl.when(jnp.logical_not(owning))(lambda: act(owners))

    def to_partner(source, target, slot):
        copy = pltpu.make_async_remote_copy(
            src_ref=source,
            dst_ref=target,
            send_sem=sems.at[slot],
            recv_sem=sems.at[slot + 1],
            device_id=partner,
            device_id_type=MESH,
        )
        copy.start()
        return copy

    def operate(turn, vector, dots, degree=None):
        first = turn == 0
        last = turn == ITERS - 1
        terms = 3 if first else 2
        base = turn * 12
        if first:
            pl.semaphore_wait(barrier, count - 1)
        vec_send[turn] = vector
        vec_copy = to_partner(vec_send.at[turn], vec_recv.at[turn], base)
        high, low = pieces(vector)
        left = jnp.concatenate([high, low], axis=0)

        def star_values(group):
            rows = gathered(cut_groups + group, left)
            for place in range(GROUP):
                chunk = group * GROUP + place
                lanes = slice(place * LANES, (place + 1) * LANES)
                sums = mm(rows8(rows[0][:, lanes], rows[1][:, lanes]), nethot[chunk], NT)
                sums = sums[0:2] + sums[2:4]
                for r in range(per_chunk):
                    send_star[turn, chunk * per_chunk + r] = sums[:, r * LANES : (r + 1) * LANES]

        over_groups(pin_groups, star_values)

        def to_owner(owner, device):
            pltpu.make_async_remote_copy(
                src_ref=send_star.at[turn, pl.ds(owner * share, share)],
                dst_ref=recv_star.at[turn, me],
                send_sem=sems.at[base + 2],
                recv_sem=sems.at[base + 3],
                device_id=device,
                device_id_type=MESH,
            ).start()

        each_owner(to_owner)

        @pl.when(owning)
        def _():
            recv_star[turn, me] = send_star[turn, pl.ds(my_share * share, share)]

        if first:
            load["cut_cell"].wait()
            over_groups(cut_groups, hot_cut)

        def cut_values(group):
            rows = gathered(group, left)
            for place in range(GROUP):
                lanes = slice(place * LANES, (place + 1) * LANES)
                send_cut[turn, group * GROUP + place] = jnp.concatenate(
                    [rows[0][:, lanes], rows[1][:, lanes]], axis=0
                )

        over_groups(cut_groups, cut_values)
        send_all(lambda other: send_cut.at[turn, other], recv_cut.at[turn], base + 8)
        recv_cut[turn, me] = send_cut[turn, me]

        if first:
            hold_blocks()
        parts = (*halves_of(high.astype(F32)), *halves_of(low.astype(F32)))
        for r, part in enumerate(parts):
            lhs_b[:, r, :LANES] = part
            lhs_b[:, r, LANES:] = part
        for tile in range(tiles):
            out = mm(lhs_b[tile].astype(BF16), quad[tile])
            pair = out[0:2] + out[2:4]
            for k in range(2):
                lanes = slice(k * LANES, (k + 1) * LANES)
                for c in range(2):
                    back[k, tile : tile + 1, c * LANES : (c + 1) * LANES] = pair[
                        c : c + 1, lanes
                    ]
                if first:
                    back[k, tile : tile + 1, 2 * LANES :] = out[4:5, lanes]
        cols = terms * LANES
        spread = jnp.zeros((span, cols), F32)
        for k in range(2):
            bh, bl = pieces(back[k, :, :cols])
            spread = spread + mm(spread_hot[k], bh) + mm(spread_hot[k], bl)
        local = [spread[:tiles, c * LANES : (c + 1) * LANES] for c in range(terms)]
        for c in range(terms):
            spr_send[turn, c * tiles : (c + 1) * tiles] = spread[
                tiles:, c * LANES : (c + 1) * LANES
            ]
        if not first:
            spr_send[turn, 2 * tiles :] = jnp.zeros((tiles, LANES), F32)
        spr_copy = to_partner(spr_send.at[turn], spr_recv.at[turn], base + 4)

        vec_copy.wait()
        other = vec_recv[turn]
        whole = [
            jnp.concatenate([vector[c * tiles : (c + 1) * tiles], other[c * tiles : (c + 1) * tiles]], axis=0)
            for c in range(2)
        ]
        wh = [pieces(x) for x in whole]
        table = jnp.concatenate([wh[0][0], wh[1][0], wh[0][1], wh[1][1]], axis=1)
        for k in range(2):
            chosen = mm(select_hot[k], table)
            for r in range(4):
                lhs_f[:, r, k * LANES : (k + 1) * LANES] = chosen[:, r * LANES : (r + 1) * LANES]
        for tile in range(tiles):
            out = mm(lhs_f[tile].astype(BF16), quad[tile], NT)
            out = out[:, :LANES] + out[:, LANES:]
            pair = out[0:2] + out[2:4]
            for c in range(2):
                front[c, tile : tile + 1, :] = pair[c : c + 1]
            if first:
                front[2, tile : tile + 1, :] = out[4:5]
        local = [local[c] + front[c] for c in range(terms)]

        if first:
            load["star_w"].wait()

        @pl.when(owning)
        def _():
            wait_all(recv_star.at[turn], base + 3)
            totals = jnp.sum(recv_star[turn], axis=0)
            weight = star_w_ref[pl.ds(my_share * share, share), :] * (1.0 / FANOUT)
            weighted = totals * weight[:, None, :]
            send2[turn] = weighted

            def send(other, device):
                pltpu.make_async_remote_copy(
                    src_ref=send2.at[turn],
                    dst_ref=recv2.at[turn, pl.ds(my_share * share, share)],
                    send_sem=sems.at[base + 6],
                    recv_sem=sems.at[base + 7],
                    device_id=device,
                    device_id_type=MESH,
                ).start()

            each_other(send)
            recv2[turn, pl.ds(my_share * share, share)] = weighted
            if last:
                star_energy[...] = jnp.sum(weighted * totals, axis=0)

        if first:
            load["cut_w"].wait()
            load["anchor"].wait()
        else:
            dots = dots()
        wait_all(recv_cut.at[turn], base + 9)
        if last:
            across = jnp.sum(
                send_cut[turn] * recv_cut[turn] * cut_w_ref[...][:, None, :], axis=0
            )
            across = across + star_energy[...]
            energy = []
            for c in range(2):
                own = vector[c * tiles : (c + 1) * tiles]
                inner = own * (degree[:tiles] * own - 2.0 * front[c])
                rows = jnp.sum(inner, axis=0, keepdims=True) - across[c : c + 1]
                energy.append(jnp.sum(rows, axis=1, keepdims=True))
            for c in range(2):
                dots = jnp.where(lane == 18 + c, energy[c], dots)
        if not first:
            dot_send[turn] = dots
            send_all(lambda other: dot_send.at[turn], dot_recv.at[turn], base + 10)
            dot_recv[turn, me] = dots

        def cut_group(group, carry):
            weights = [cut_w_ref[pl.ds(group * GROUP + p, 1), :] for p in range(GROUP)]
            weight = jnp.concatenate(weights, axis=1)
            rows = [
                jnp.concatenate(
                    [recv_cut[turn, group * GROUP + p, c : c + 1, :] for p in range(GROUP)], axis=1
                )
                * weight
                for c in range(2)
            ]
            if first:
                rows.append(weight)
            return carry + scattered(group, rows)

        total = sum_groups(cut_groups, cut_group, jnp.zeros((terms * tiles, LANES), F32))

        def pin_weights(group, carry):
            row = []
            for place in range(GROUP):
                chunk = group * GROUP + place
                parts = [chunk * per_chunk + r for r in range(per_chunk)]
                own = jnp.concatenate([star_w_ref[pl.ds(o, 1), :] for o in parts], axis=1)
                got = mm(rows8(own, own), nethot[chunk])
                row.append(got[0:1] + got[2:3])
            return carry + scattered(cut_groups + group, [jnp.concatenate(row, axis=1)])

        if first:
            weighed = sum_groups(pin_groups, pin_weights, total[2 * tiles :])
        spr_copy.wait()
        for_owner(lambda n: wait_all(recv2.at[turn], base + 7, n * share))

        def pin_group(group, carry):
            rows = [[], []]
            for place in range(GROUP):
                chunk = group * GROUP + place
                parts = [chunk * per_chunk + r for r in range(per_chunk)]
                table = [
                    jnp.concatenate([recv2[turn, o, c : c + 1, :] for o in parts], axis=1)
                    for c in range(2)
                ]
                got = mm(rows8(*table), nethot[chunk])
                got = got[0:2] + got[2:4]
                for c in range(2):
                    rows[c].append(got[c : c + 1])
            return carry + scattered(
                cut_groups + group, [jnp.concatenate(r, axis=1) for r in rows]
            )

        total = sum_groups(pin_groups, pin_group, total[: 2 * tiles])
        if first:
            total = jnp.concatenate([total, weighed], axis=0)
        arrived = spr_recv[turn]
        both = jnp.concatenate(local, axis=0) + arrived[: terms * tiles] + total
        summed = None
        if not first:
            wait_all(dot_recv.at[turn], base + 11)
            summed = jnp.sum(dot_recv[turn], axis=0)
            wait_all(dot_recv.at[turn], base + 10)
        for_owner(lambda n: wait_all(send_star.at[turn], base + 2, n * share))
        wait_all(send_cut.at[turn], base + 8)

        @pl.when(owning)
        def _():
            wait_all(recv_star.at[turn], base + 6)

        return both, summed

    def pick(row, k):
        return jnp.sum(jnp.where(lane == k, row, 0.0), axis=1, keepdims=True)

    def stretch(pair):
        return jnp.concatenate(
            [jnp.broadcast_to(x, (tiles, LANES)) for x in pair], axis=0
        )

    def dots_of(pairs):
        return dot_rows([both for a, b in pairs for both in zip(halves_of(a), halves_of(b))])

    load["rs"].wait()
    r = jnp.concatenate(
        [
            rs_ref[c : c + 1, t * LANES : (t + 1) * LANES]
            for c in range(2)
            for t in range(tiles)
        ],
        axis=0,
    )
    both, _ = operate(0, r, None)
    degree = anchor_ref[...] + both[2 * tiles :]
    degree = jnp.concatenate([degree, degree], axis=0)
    w = degree * r - both[: 2 * tiles]
    x = jnp.zeros_like(r)
    p = s = z = None
    old_gamma = old_alpha = old_beta = beta = None
    for iteration in range(ITERS):
        if iteration + 1 < ITERS:
            pairs = [(r, r), (w, r)]
            if iteration + 2 == ITERS:
                pairs += [(r, s), (w, w), (w, s), (s, s), (w, z), (z, r), (z, s)]
            both, summed = operate(iteration + 1, w, functools.partial(dots_of, pairs), degree)
            q = degree * w - both
            gamma = [pick(summed, c) for c in range(2)]
            delta = [pick(summed, 2 + c) for c in range(2)]
        else:
            gamma, delta = [], []
            for c in range(2):
                rr, wr, rs, ww, ws, ss, wz, zr, zs, wq = [
                    pick(summed, 2 * k + c) for k in range(10)
                ]
                a, b = old_alpha[c], old_beta[c]
                ws_part = ww + b * ws
                gamma.append(
                    rr - 2.0 * a * (wr + b * rs) + a * a * (ws_part + b * (ws + b * ss))
                )
                w_next = wr - a * ws_part
                q_next = ww - a * (wq + b * wz)
                z_next = zr - a * (wz + b * zs)
                delta.append(w_next - a * (q_next + b * z_next))
        if iteration == 0:
            alpha = [gamma[c] / delta[c] for c in range(2)]
            p, s = r, w
            if iteration + 1 < ITERS:
                z = q
        else:
            beta = [gamma[c] / old_gamma[c] for c in range(2)]
            alpha = [
                gamma[c] / (delta[c] - beta[c] * gamma[c] / old_alpha[c]) for c in range(2)
            ]
            spread_beta = stretch(beta)
            p = r + spread_beta * p
            s = w + spread_beta * s
            if iteration + 1 < ITERS:
                z = q + spread_beta * z
        step = stretch(alpha)
        x = x + step * p
        r = r - step * s
        if iteration + 1 < ITERS:
            w = w - step * z
        old_gamma, old_alpha, old_beta = gamma, alpha, beta
    for c in range(2):
        for t in range(tiles):
            row = c * tiles + t
            lanes = slice(t * LANES, (t + 1) * LANES)
            out_ref[c : c + 1, lanes] = x[row : row + 1]
            out_ref[2 + c : 3 + c, lanes] = r[row : row + 1]


def per_device(
    regions,
    halves,
    right_side,
    anchor,
    blocks,
    tile_nbr,
    cut_cells,
    cut_weight,
    pin_cell,
    pin_net,
    star_weight,
):
    count = regions * halves
    tiles = blocks.shape[0]
    near = blocks.shape[1]
    pin_chunks = pin_cell.shape[0] // LANES
    per_chunk = count // pin_chunks
    groups = count // GROUP + pin_chunks // GROUP
    wide = GROUP * LANES
    share = count // ((regions - 2 * (regions // 4)) * halves)
    vmem = pl.BlockSpec(memory_space=pltpu.VMEM)
    shape = jax.ShapeDtypeStruct((4, tiles * LANES), F32)
    joint = pl.pallas_call(
        functools.partial(kernel, regions, halves),
        out_shape=shape,
        in_specs=[pl.BlockSpec(memory_space=pl.ANY)] * 9,
        out_specs=vmem,
        scratch_shapes=[
            pltpu.VMEM(right_side.shape, F32),
            pltpu.VMEM((tiles, LANES), F32),
            pltpu.VMEM((near, tiles), jnp.int32),
            pltpu.VMEM((count, LANES), jnp.int32),
            pltpu.VMEM((count, LANES), F32),
            pltpu.VMEM((pin_chunks, LANES), jnp.int32),
            pltpu.VMEM((pin_chunks, LANES), jnp.int32),
            pltpu.VMEM((count, LANES), F32),
            pltpu.VMEM((groups, LANES, wide), BF16),
            pltpu.VMEM((groups, tiles, wide), F32),
            pltpu.VMEM((tiles * near, LANES, LANES), F32),
            pltpu.VMEM((pin_chunks, per_chunk * LANES, LANES), BF16),
            pltpu.VMEM((tiles, 2 * LANES, 2 * LANES), BF16),
            pltpu.VMEM((tiles, 8, 2 * LANES), F32),
            pltpu.VMEM((tiles, 8, 2 * LANES), F32),
            pltpu.VMEM((2, tiles, 3 * LANES), F32),
            pltpu.VMEM((3, tiles, LANES), F32),
            pltpu.VMEM((ITERS, count, 2, LANES), F32),
            pltpu.VMEM((ITERS, count, share, 2, LANES), F32),
            pltpu.VMEM((ITERS, count, 2, LANES), F32),
            pltpu.VMEM((ITERS, count, 2, LANES), F32),
            pltpu.VMEM((ITERS, share, 2, LANES), F32),
            pltpu.VMEM((ITERS, count, 2, LANES), F32),
            pltpu.VMEM((ITERS, 1, LANES), F32),
            pltpu.VMEM((ITERS, count, 1, LANES), F32),
            pltpu.VMEM((2, LANES), F32),
            pltpu.VMEM((ITERS, 2 * tiles, LANES), F32),
            pltpu.VMEM((ITERS, 2 * tiles, LANES), F32),
            pltpu.VMEM((ITERS, 3 * tiles, LANES), F32),
            pltpu.VMEM((ITERS, 3 * tiles, LANES), F32),
            pltpu.SemaphoreType.DMA((12 * ITERS,)),
            pltpu.SemaphoreType.DMA((9,)),
        ],
        compiler_params=pltpu.CompilerParams(
            collective_id=0, has_side_effects=True, vmem_limit_bytes=56 * 1024 * 1024
        ),
    )(
        right_side,
        anchor.reshape(tiles, LANES),
        blocks.reshape(tiles * near, LANES, LANES),
        tile_nbr.T,
        cut_cells[0],
        cut_weight[0],
        pin_cell.reshape(pin_chunks, LANES),
        pin_net.reshape(pin_chunks, LANES),
        star_weight.reshape(count, LANES),
    )
    return joint[:2], joint[2:]


def solution(mesh):
    return jax.shard_map(
        functools.partial(per_device, mesh.shape["region"], mesh.shape["coord"]),
        mesh=mesh,
        in_specs=(
            P(None, ("region", "coord")),
            P(("region", "coord")),
            P(("region", "coord"), None, None, None),
            P(("region", "coord"), None),
            P(("region", "coord"), None, None),
            P(("region", "coord"), None, None),
            P(("region", "coord")),
            P(("region", "coord")),
            P(),
        ),
        out_specs=(P(None, ("region", "coord")), P(None, ("region", "coord"))),
        check_vma=False,
    )
```

```python
import functools

import jax
import jax.numpy as jnp
from jax import lax
from jax.experimental import pallas as pl
from jax.experimental.pallas import tpu as pltpu
from jax.sharding import PartitionSpec as P

FANOUT = 32
ITERS = 3
LANES = 128
GROUP = 4
MESH = pl.DeviceIdType.MESH
F32 = jnp.float32
BF16 = jnp.bfloat16

NN = (((1,), (0,)), ((), ()))
NT = (((1,), (1,)), ((), ()))


def mm(a, b, dims=NN):
    return lax.dot_general(a, b, dims, preferred_element_type=F32)


def pieces(x):
    high = x.astype(BF16)
    low = (x - high.astype(F32)).astype(BF16)
    return high, low


def kernel(
    regions,
    halves,
    rs_hbm,
    anchor_hbm,
    blocks_ref,
    nbr_row_hbm,
    cut_cell_hbm,
    cut_w_hbm,
    pin_cell_hbm,
    pin_net_hbm,
    star_w_hbm,
    out_ref,
    rs_ref,
    anchor_ref,
    nbr_row_ref,
    cut_cell_ref,
    cut_w_ref,
    pin_cell_ref,
    pin_net_ref,
    star_w_ref,
    onehot,
    himask,
    block_buf,
    nethot,
    quad,
    lhs_b,
    lhs_f,
    back,
    front,
    send_star,
    recv_star,
    send_cut,
    recv_cut,
    send2,
    recv2,
    dot_send,
    dot_recv,
    star_energy,
    vec_send,
    vec_recv,
    spr_send,
    spr_recv,
    sems,
    in_sems,
):
    count = regions * halves
    first_owner = regions // 4
    owner_regions = regions - 2 * first_owner
    owners = owner_regions * halves
    share = count // owners
    tiles = anchor_ref.shape[0]
    cut_groups = count // GROUP
    pin_chunks = pin_cell_ref.shape[0]
    pin_groups = pin_chunks // GROUP
    per_chunk = count // pin_chunks
    wide = GROUP * LANES
    my_region = lax.axis_index("region")
    my_half = lax.axis_index("coord")
    me = my_region * halves + my_half
    partner = (my_region, 1 - my_half)
    owning = jnp.logical_and(my_region >= first_owner, my_region < first_owner + owner_regions)
    my_share = (my_region - first_owner) * halves + my_half

    def each_other(act):
        act(my_region * halves + 1 - my_half, partner)

        @pl.loop(1, regions, unroll=True if regions <= 16 else 4)
        def _(step):
            region = my_region + step
            region = jnp.where(region >= regions, region - regions, region)
            for flip in range(halves):
                half = my_half if flip == 0 else 1 - my_half
                act(region * halves + half, (region, half))

    half_owners = owner_regions // 2
    regions_per_group = owner_regions // pin_groups
    farthest = half_owners - 1 - lax.rem(my_region, half_owners)
    farthest = farthest + jnp.where(my_region < regions // 2, half_owners, 0)
    farthest = farthest // regions_per_group

    def far_first(step):
        group = 0
        bit = 1
        while bit < pin_groups:
            group = group + lax.rem(farthest // bit + step // bit, 2) * bit
            bit *= 2
        return group

    def over_groups(groups, body):
        if groups <= 8:
            for group in range(groups):
                body(group)
        else:
            pl.loop(0, groups, unroll=4)(body)

    def sum_groups(groups, body, total):
        if groups <= 8:
            for group in range(groups):
                total = body(group, total)
            return total
        return lax.fori_loop(0, groups, body, total, unroll=4)

    barrier = pltpu.get_barrier_semaphore()

    def greet(other, device):
        pl.semaphore_signal(barrier, inc=1, device_id=device, device_id_type=MESH)

    each_other(greet)
    load = {}
    for k, (name, source, target) in enumerate(
        (
            ("pin_cell", pin_cell_hbm, pin_cell_ref),
            ("pin_net", pin_net_hbm, pin_net_ref),
            ("rs", rs_hbm, rs_ref),
            ("cut_cell", cut_cell_hbm, cut_cell_ref),
            ("nbr", nbr_row_hbm, nbr_row_ref),
            ("star_w", star_w_hbm, star_w_ref),
            ("cut_w", cut_w_hbm, cut_w_ref),
            ("anchor", anchor_hbm, anchor_ref),
            ("blocks", blocks_ref, block_buf),
        )
    ):
        load[name] = pltpu.make_async_copy(source, target, in_sems.at[k])
        load[name].start()
    star_energy[...] = jnp.zeros_like(star_energy)

    iota_lo = lax.broadcasted_iota(jnp.int32, (LANES, LANES), 0)
    iota_hi = lax.broadcasted_iota(jnp.int32, (tiles, LANES), 0)
    iota_net = lax.broadcasted_iota(jnp.int32, (per_chunk * LANES, LANES), 0)
    lane = lax.broadcasted_iota(jnp.int32, (1, LANES), 1)

    def put_onehot(group, place, cells):
        lanes = slice(place * LANES, (place + 1) * LANES)
        low = lax.bitwise_and(cells, LANES - 1)
        high = lax.shift_right_logical(cells, 7)
        onehot[group, :, lanes] = (iota_lo == low).astype(F32).astype(BF16)
        himask[group, :, lanes] = (iota_hi == high).astype(F32)

    def hot_pins(group):
        for place in range(GROUP):
            chunk = group * GROUP + place
            put_onehot(cut_groups + group, place, pin_cell_ref[pl.ds(chunk, 1), :])
            net = pin_net_ref[pl.ds(chunk, 1), :] - chunk * (per_chunk * LANES)
            nethot[chunk] = (iota_net == net).astype(F32).astype(BF16)

    def hot_cut(group):
        for place in range(GROUP):
            put_onehot(group, place, cut_cell_ref[pl.ds(group * GROUP + place, 1), :])

    load["pin_cell"].wait()
    load["pin_net"].wait()
    over_groups(pin_groups, hot_pins)

    def hold_blocks():
        load["blocks"].wait()

        @pl.loop(0, tiles, unroll=4)
        def _(tile):
            for k in range(2):
                high, low = pieces(block_buf[2 * tile + k])
                lanes = slice(k * LANES, (k + 1) * LANES)
                quad[tile, :LANES, lanes] = high
                quad[tile, LANES:, lanes] = low

        ones_row = jnp.where(lax.broadcasted_iota(jnp.int32, (8, 2 * LANES), 0) == 4, 1.0, 0.0)
        for tile in range(tiles):
            lhs_b[tile] = ones_row
            lhs_f[tile] = ones_row

    load["nbr"].wait()
    shift = my_half * tiles
    span = 2 * tiles
    rel_row = nbr_row_ref[...] - shift
    rel_row = jnp.where(rel_row < 0, rel_row + span, rel_row)
    on_diagonal = lax.broadcasted_iota(jnp.int32, (tiles, tiles), 0) == lax.broadcasted_iota(
        jnp.int32, (tiles, tiles), 1
    )
    rel_col = [
        jnp.sum(
            jnp.where(on_diagonal, rel_row[k : k + 1, :].astype(F32), 0.0), axis=1, keepdims=True
        ).astype(jnp.int32)
        for k in range(2)
    ]
    spread_hot = [
        (lax.broadcasted_iota(jnp.int32, (span, tiles), 0) == rel_row[k : k + 1, :])
        .astype(F32)
        .astype(BF16)
        for k in range(2)
    ]
    select_hot = [
        (lax.broadcasted_iota(jnp.int32, (tiles, span), 1) == rel_col[k])
        .astype(F32)
        .astype(BF16)
        for k in range(2)
    ]

    def rows8(first, second):
        fh, fl = pieces(first)
        sh, sl = pieces(second)
        stacked = jnp.concatenate(
            [x.astype(F32) for x in (fh, sh, fl, sl)]
            + [jnp.zeros((4, first.shape[1]), F32)],
            axis=0,
        )
        return stacked.astype(BF16)

    sub = lax.broadcasted_iota(jnp.int32, (8, wide), 0)
    in_half = sub < 4
    in_pair = lax.rem(sub, 4) < 2

    def fold_tiles(rows, mask):
        rows = rows * mask
        total = rows[:8]
        for t in range(8, tiles, 8):
            total = total + rows[t : t + 8]
        return total

    def fold_two(a, b):
        return jnp.where(in_half, a, b) + pltpu.roll(jnp.where(in_half, b, a), 4, 0)

    def gathered(group, left):
        got = mm(left, onehot[group])
        got = got[: 2 * tiles] + got[2 * tiles :]
        mask = himask[group]
        both = fold_two(fold_tiles(got[:tiles], mask), fold_tiles(got[tiles:], mask))
        both = both + pltpu.roll(both, 6, 0)
        both = both + pltpu.roll(both, 7, 0)
        return both[0:1], both[4:5]

    def gathered_pieces(group, left):
        got = mm(left, onehot[group])
        mask = himask[group]
        part = [fold_tiles(got[k * tiles : (k + 1) * tiles], mask) for k in range(4)]
        high = fold_two(part[0], part[1])
        low = fold_two(part[2], part[3])
        both = jnp.where(in_pair, high + pltpu.roll(high, 6, 0), low + pltpu.roll(low, 2, 0))
        return (both + pltpu.roll(both, 7, 0)).astype(BF16)

    def scattered(group, rows):
        mask = himask[group]
        spread = jnp.concatenate([mask * row for row in rows], axis=0)
        high, low = pieces(spread)
        both = mm(jnp.concatenate([high, low], axis=0), onehot[group], NT)
        rows_all = len(rows) * tiles
        return both[:rows_all] + both[rows_all:]

    def dot_rows(values):
        row = jnp.zeros((1, LANES), F32)
        for k, (a, b) in enumerate(values):
            total = jnp.sum(jnp.sum(a * b, axis=0, keepdims=True), axis=1, keepdims=True)
            row = jnp.where(lane == k, total, row)
        return row

    def halves_of(x):
        return x[:tiles], x[tiles:]

    def send_all(source_of, target, slot):
        def send(other, device):
            pltpu.make_async_remote_copy(
                src_ref=source_of(other),
                dst_ref=target.at[me],
                send_sem=sems.at[slot],
                recv_sem=sems.at[slot + 1],
                device_id=device,
                device_id_type=MESH,
            ).start()

        each_other(send)

    def wait_all(like, slot, messages=count - 1):
        part = like.at[pl.ds(0, messages)]
        pltpu.make_async_copy(part, part, sems.at[slot]).wait()

    def for_owner(act):
        pl.when(owning)(lambda: act(owners - 1))
        pl.when(jnp.logical_not(owning))(lambda: act(owners))

    def to_partner(source, target, slot):
        copy = pltpu.make_async_remote_copy(
            src_ref=source,
            dst_ref=target,
            send_sem=sems.at[slot],
            recv_sem=sems.at[slot + 1],
            device_id=partner,
            device_id_type=MESH,
        )
        copy.start()
        return copy

    def operate(turn, vector, dots, degree=None):
        first = turn == 0
        last = turn == ITERS - 1
        terms = 3 if first else 2
        base = turn * 12
        vec_send[turn] = vector
        if not first:
            vec_copy = to_partner(vec_send.at[turn], vec_recv.at[turn], base)
        high, low = pieces(vector)
        left = jnp.concatenate([high, low], axis=0)

        def star_values(group):
            rows = gathered_pieces(cut_groups + group, left)
            for place in range(GROUP):
                chunk = group * GROUP + place
                sums = mm(rows[:, place * LANES : (place + 1) * LANES], nethot[chunk], NT)
                sums = sums + pltpu.roll(sums, 6, 0)
                for r in range(per_chunk):
                    lanes = slice(r * LANES, (r + 1) * LANES)
                    for c in range(2):
                        send_star[turn, chunk * per_chunk + r, c : c + 1] = sums[
                            4 * c : 4 * c + 1, lanes
                        ]

        def to_owner(owner, device):
            pltpu.make_async_remote_copy(
                src_ref=send_star.at[turn, pl.ds(owner * share, share)],
                dst_ref=recv_star.at[turn, me],
                send_sem=sems.at[base + 2],
                recv_sem=sems.at[base + 3],
                device_id=device,
                device_id_type=MESH,
            ).start()

        def to_owners_of(group, nearest):
            for k in range(regions_per_group):
                place = group * regions_per_group + k
                act = functools.partial(to_owner, place * halves + my_half)
                device = (place + first_owner, my_half)
                to_owner(place * halves + 1 - my_half, (place + first_owner, 1 - my_half))
                if nearest:
                    pl.when(place + first_owner != my_region)(functools.partial(act, device))
                else:
                    act(device)

        over_groups(pin_groups, star_values)
        if first:
            pl.semaphore_wait(barrier, count - 1)
        for step in range(pin_groups):
            to_owners_of(far_first(step), step + 1 == pin_groups)

        @pl.when(owning)
        def _():
            recv_star[turn, me] = send_star[turn, pl.ds(my_share * share, share)]

        if first:
            vec_copy = to_partner(vec_send.at[turn], vec_recv.at[turn], base)
            load["cut_cell"].wait()
            over_groups(cut_groups, hot_cut)

        def cut_values(group):
            rows = gathered(group, left)
            for place in range(GROUP):
                lanes = slice(place * LANES, (place + 1) * LANES)
                send_cut[turn, group * GROUP + place] = jnp.concatenate(
                    [rows[0][:, lanes], rows[1][:, lanes]], axis=0
                )

        over_groups(cut_groups, cut_values)
        send_all(lambda other: send_cut.at[turn, other], recv_cut.at[turn], base + 8)
        recv_cut[turn, me] = send_cut[turn, me]

        if first:
            hold_blocks()
        parts = (*halves_of(high.astype(F32)), *halves_of(low.astype(F32)))
        for r, part in enumerate(parts):
            lhs_b[:, r, :LANES] = part
            lhs_b[:, r, LANES:] = part
        for tile in range(tiles):
            out = mm(lhs_b[tile].astype(BF16), quad[tile])
            pair = out[0:2] + out[2:4]
            for k in range(2):
                lanes = slice(k * LANES, (k + 1) * LANES)
                for c in range(2):
                    back[k, tile : tile + 1, c * LANES : (c + 1) * LANES] = pair[
                        c : c + 1, lanes
                    ]
                if first:
                    back[k, tile : tile + 1, 2 * LANES :] = out[4:5, lanes]
        cols = terms * LANES
        spread = jnp.zeros((span, cols), F32)
        for k in range(2):
            bh, bl = pieces(back[k, :, :cols])
            spread = spread + mm(spread_hot[k], bh) + mm(spread_hot[k], bl)
        local = [spread[:tiles, c * LANES : (c + 1) * LANES] for c in range(terms)]
        for c in range(terms):
            spr_send[turn, c * tiles : (c + 1) * tiles] = spread[
                tiles:, c * LANES : (c + 1) * LANES
            ]
        if not first:
            spr_send[turn, 2 * tiles :] = jnp.zeros((tiles, LANES), F32)
        spr_copy = to_partner(spr_send.at[turn], spr_recv.at[turn], base + 4)

        vec_copy.wait()
        other = vec_recv[turn]
        whole = [
            jnp.concatenate([vector[c * tiles : (c + 1) * tiles], other[c * tiles : (c + 1) * tiles]], axis=0)
            for c in range(2)
        ]
        wh = [pieces(x) for x in whole]
        table = jnp.concatenate([wh[0][0], wh[1][0], wh[0][1], wh[1][1]], axis=1)
        for k in range(2):
            chosen = mm(select_hot[k], table)
            for r in range(4):
                lhs_f[:, r, k * LANES : (k + 1) * LANES] = chosen[:, r * LANES : (r + 1) * LANES]
        for tile in range(tiles):
            out = mm(lhs_f[tile].astype(BF16), quad[tile], NT)
            out = out[:, :LANES] + out[:, LANES:]
            pair = out[0:2] + out[2:4]
            for c in range(2):
                front[c, tile : tile + 1, :] = pair[c : c + 1]
            if first:
                front[2, tile : tile + 1, :] = out[4:5]
        local = [local[c] + front[c] for c in range(terms)]

        if first:
            load["star_w"].wait()

        @pl.when(owning)
        def _():
            wait_all(recv_star.at[turn], base + 3)
            totals = jnp.sum(recv_star[turn], axis=0)
            weight = star_w_ref[pl.ds(my_share * share, share), :] * (1.0 / FANOUT)
            weighted = totals * weight[:, None, :]
            send2[turn] = weighted

            def send(other, device):
                pltpu.make_async_remote_copy(
                    src_ref=send2.at[turn],
                    dst_ref=recv2.at[turn, pl.ds(my_share * share, share)],
                    send_sem=sems.at[base + 6],
                    recv_sem=sems.at[base + 7],
                    device_id=device,
                    device_id_type=MESH,
                ).start()

            each_other(send)
            recv2[turn, pl.ds(my_share * share, share)] = weighted
            if last:
                star_energy[...] = jnp.sum(weighted * totals, axis=0)

        if first:
            load["cut_w"].wait()
            load["anchor"].wait()
        else:
            dots = dots()
        wait_all(recv_cut.at[turn], base + 9)
        if last:
            across = jnp.sum(
                send_cut[turn] * recv_cut[turn] * cut_w_ref[...][:, None, :], axis=0
            )
            across = across + star_energy[...]
            energy = []
            for c in range(2):
                own = vector[c * tiles : (c + 1) * tiles]
                inner = own * (degree[:tiles] * own - 2.0 * front[c])
                rows = jnp.sum(inner, axis=0, keepdims=True) - across[c : c + 1]
                energy.append(jnp.sum(rows, axis=1, keepdims=True))
            for c in range(2):
                dots = jnp.where(lane == 18 + c, energy[c], dots)
        if not first:
            dot_send[turn] = dots
            send_all(lambda other: dot_send.at[turn], dot_recv.at[turn], base + 10)
            dot_recv[turn, me] = dots

        def cut_group(group, carry):
            weights = [cut_w_ref[pl.ds(group * GROUP + p, 1), :] for p in range(GROUP)]
            weight = jnp.concatenate(weights, axis=1)
            rows = [
                jnp.concatenate(
                    [recv_cut[turn, group * GROUP + p, c : c + 1, :] for p in range(GROUP)], axis=1
                )
                * weight
                for c in range(2)
            ]
            if first:
                rows.append(weight)
            return carry + scattered(group, rows)

        total = sum_groups(cut_groups, cut_group, jnp.zeros((terms * tiles, LANES), F32))

        def pin_weights(group, carry):
            row = []
            for place in range(GROUP):
                chunk = group * GROUP + place
                parts = [chunk * per_chunk + r for r in range(per_chunk)]
                own = jnp.concatenate([star_w_ref[pl.ds(o, 1), :] for o in parts], axis=1)
                got = mm(rows8(own, own), nethot[chunk])
                row.append(got[0:1] + got[2:3])
            return carry + scattered(cut_groups + group, [jnp.concatenate(row, axis=1)])

        if first:
            weighed = sum_groups(pin_groups, pin_weights, total[2 * tiles :])
        spr_copy.wait()
        for_owner(lambda n: wait_all(recv2.at[turn], base + 7, n * share))

        def pin_group(group, carry):
            rows = [[], []]
            for place in range(GROUP):
                chunk = group * GROUP + place
                parts = [chunk * per_chunk + r for r in range(per_chunk)]
                table = [
                    jnp.concatenate([recv2[turn, o, c : c + 1, :] for o in parts], axis=1)
                    for c in range(2)
                ]
                got = mm(rows8(*table), nethot[chunk])
                got = got[0:2] + got[2:4]
                for c in range(2):
                    rows[c].append(got[c : c + 1])
            return carry + scattered(
                cut_groups + group, [jnp.concatenate(r, axis=1) for r in rows]
            )

        total = sum_groups(pin_groups, pin_group, total[: 2 * tiles])
        if first:
            total = jnp.concatenate([total, weighed], axis=0)
        arrived = spr_recv[turn]
        both = jnp.concatenate(local, axis=0) + arrived[: terms * tiles] + total
        summed = None
        if not first:
            wait_all(dot_recv.at[turn], base + 11)
            summed = jnp.sum(dot_recv[turn], axis=0)
            wait_all(dot_recv.at[turn], base + 10)
        for_owner(lambda n: wait_all(send_star.at[turn], base + 2, n * share))
        wait_all(send_cut.at[turn], base + 8)

        @pl.when(owning)
        def _():
            wait_all(recv_star.at[turn], base + 6)

        return both, summed

    def pick(row, k):
        return jnp.sum(jnp.where(lane == k, row, 0.0), axis=1, keepdims=True)

    def stretch(pair):
        return jnp.concatenate(
            [jnp.broadcast_to(x, (tiles, LANES)) for x in pair], axis=0
        )

    def dots_of(pairs):
        return dot_rows([both for a, b in pairs for both in zip(halves_of(a), halves_of(b))])

    load["rs"].wait()
    r = jnp.concatenate(
        [
            rs_ref[c : c + 1, t * LANES : (t + 1) * LANES]
            for c in range(2)
            for t in range(tiles)
        ],
        axis=0,
    )
    both, _ = operate(0, r, None)
    degree = anchor_ref[...] + both[2 * tiles :]
    degree = jnp.concatenate([degree, degree], axis=0)
    w = degree * r - both[: 2 * tiles]
    x = jnp.zeros_like(r)
    p = s = z = None
    old_gamma = old_alpha = old_beta = beta = None
    for iteration in range(ITERS):
        if iteration + 1 < ITERS:
            pairs = [(r, r), (w, r)]
            if iteration + 2 == ITERS:
                pairs += [(r, s), (w, w), (w, s), (s, s), (w, z), (z, r), (z, s)]
            both, summed = operate(iteration + 1, w, functools.partial(dots_of, pairs), degree)
            q = degree * w - both
            gamma = [pick(summed, c) for c in range(2)]
            delta = [pick(summed, 2 + c) for c in range(2)]
        else:
            gamma, delta = [], []
            for c in range(2):
                rr, wr, rs, ww, ws, ss, wz, zr, zs, wq = [
                    pick(summed, 2 * k + c) for k in range(10)
                ]
                a, b = old_alpha[c], old_beta[c]
                ws_part = ww + b * ws
                gamma.append(
                    rr - 2.0 * a * (wr + b * rs) + a * a * (ws_part + b * (ws + b * ss))
                )
                w_next = wr - a * ws_part
                q_next = ww - a * (wq + b * wz)
                z_next = zr - a * (wz + b * zs)
                delta.append(w_next - a * (q_next + b * z_next))
        if iteration == 0:
            alpha = [gamma[c] / delta[c] for c in range(2)]
            p, s = r, w
            if iteration + 1 < ITERS:
                z = q
        else:
            beta = [gamma[c] / old_gamma[c] for c in range(2)]
            alpha = [
                gamma[c] / (delta[c] - beta[c] * gamma[c] / old_alpha[c]) for c in range(2)
            ]
            spread_beta = stretch(beta)
            p = r + spread_beta * p
            s = w + spread_beta * s
            if iteration + 1 < ITERS:
                z = q + spread_beta * z
        step = stretch(alpha)
        x = x + step * p
        r = r - step * s
        if iteration + 1 < ITERS:
            w = w - step * z
        old_gamma, old_alpha, old_beta = gamma, alpha, beta
    for c in range(2):
        for t in range(tiles):
            row = c * tiles + t
            lanes = slice(t * LANES, (t + 1) * LANES)
            out_ref[c : c + 1, lanes] = x[row : row + 1]
            out_ref[2 + c : 3 + c, lanes] = r[row : row + 1]


def per_device(
    regions,
    halves,
    right_side,
    anchor,
    blocks,
    tile_nbr,
    cut_cells,
    cut_weight,
    pin_cell,
    pin_net,
    star_weight,
):
    count = regions * halves
    tiles = blocks.shape[0]
    near = blocks.shape[1]
    pin_chunks = pin_cell.shape[0] // LANES
    per_chunk = count // pin_chunks
    groups = count // GROUP + pin_chunks // GROUP
    wide = GROUP * LANES
    share = count // ((regions - 2 * (regions // 4)) * halves)
    vmem = pl.BlockSpec(memory_space=pltpu.VMEM)
    shape = jax.ShapeDtypeStruct((4, tiles * LANES), F32)
    joint = pl.pallas_call(
        functools.partial(kernel, regions, halves),
        out_shape=shape,
        in_specs=[pl.BlockSpec(memory_space=pltpu.HBM)] * 9,
        out_specs=vmem,
        scratch_shapes=[
            pltpu.VMEM(right_side.shape, F32),
            pltpu.VMEM((tiles, LANES), F32),
            pltpu.VMEM((near, tiles), jnp.int32),
            pltpu.VMEM((count, LANES), jnp.int32),
            pltpu.VMEM((count, LANES), F32),
            pltpu.VMEM((pin_chunks, LANES), jnp.int32),
            pltpu.VMEM((pin_chunks, LANES), jnp.int32),
            pltpu.VMEM((count, LANES), F32),
            pltpu.VMEM((groups, LANES, wide), BF16),
            pltpu.VMEM((groups, tiles, wide), F32),
            pltpu.VMEM((tiles * near, LANES, LANES), F32),
            pltpu.VMEM((pin_chunks, per_chunk * LANES, LANES), BF16),
            pltpu.VMEM((tiles, 2 * LANES, 2 * LANES), BF16),
            pltpu.VMEM((tiles, 8, 2 * LANES), F32),
            pltpu.VMEM((tiles, 8, 2 * LANES), F32),
            pltpu.VMEM((2, tiles, 3 * LANES), F32),
            pltpu.VMEM((3, tiles, LANES), F32),
            pltpu.VMEM((ITERS, count, 2, LANES), F32),
            pltpu.VMEM((ITERS, count, share, 2, LANES), F32),
            pltpu.VMEM((ITERS, count, 2, LANES), F32),
            pltpu.VMEM((ITERS, count, 2, LANES), F32),
            pltpu.VMEM((ITERS, share, 2, LANES), F32),
            pltpu.VMEM((ITERS, count, 2, LANES), F32),
            pltpu.VMEM((ITERS, 1, LANES), F32),
            pltpu.VMEM((ITERS, count, 1, LANES), F32),
            pltpu.VMEM((2, LANES), F32),
            pltpu.VMEM((ITERS, 2 * tiles, LANES), F32),
            pltpu.VMEM((ITERS, 2 * tiles, LANES), F32),
            pltpu.VMEM((ITERS, 3 * tiles, LANES), F32),
            pltpu.VMEM((ITERS, 3 * tiles, LANES), F32),
            pltpu.SemaphoreType.DMA((12 * ITERS,)),
            pltpu.SemaphoreType.DMA((9,)),
        ],
        compiler_params=pltpu.CompilerParams(
            collective_id=0, has_side_effects=True, vmem_limit_bytes=24 * 1024 * 1024
        ),
    )(*[pltpu.with_memory_space_constraint(v, pltpu.HBM) for v in (
        right_side,
        anchor.reshape(tiles, LANES),
        blocks.reshape(tiles * near, LANES, LANES),
        tile_nbr.T,
        cut_cells[0],
        cut_weight[0],
        pin_cell.reshape(pin_chunks, LANES),
        pin_net.reshape(pin_chunks, LANES),
        star_weight.reshape(count, LANES),
    )])
    return joint[:2], joint[2:]


def solution(mesh):
    return jax.shard_map(
        functools.partial(per_device, mesh.shape["region"], mesh.shape["coord"]),
        mesh=mesh,
        in_specs=(
            P(None, ("region", "coord")),
            P(("region", "coord")),
            P(("region", "coord"), None, None, None),
            P(("region", "coord"), None),
            P(("region", "coord"), None, None),
            P(("region", "coord"), None, None),
            P(("region", "coord")),
            P(("region", "coord")),
            P(),
        ),
        out_specs=(P(None, ("region", "coord")), P(None, ("region", "coord"))),
        check_vma=False,
    )
```

```python
import functools

import jax
import jax.numpy as jnp
from jax import lax
from jax.experimental import pallas as pl
from jax.experimental.pallas import tpu as pltpu
from jax.sharding import PartitionSpec as P

FANOUT = 32
ITERS = 3
LANES = 128
GROUP = 4
MESH = pl.DeviceIdType.MESH
F32 = jnp.float32
BF16 = jnp.bfloat16

NN = (((1,), (0,)), ((), ()))
NT = (((1,), (1,)), ((), ()))


def mm(a, b, dims=NN):
    return lax.dot_general(a, b, dims, preferred_element_type=F32)


def pieces(x):
    high = x.astype(BF16)
    low = (x - high.astype(F32)).astype(BF16)
    return high, low


def kernel(
    regions,
    halves,
    rs_hbm,
    anchor_hbm,
    blocks_ref,
    nbr_row_hbm,
    cut_cell_hbm,
    cut_w_hbm,
    pin_cell_hbm,
    pin_net_hbm,
    star_w_hbm,
    out_ref,
    rs_ref,
    anchor_ref,
    nbr_row_ref,
    cut_cell_ref,
    cut_w_ref,
    pin_cell_ref,
    pin_net_ref,
    star_w_ref,
    onehot,
    himask,
    block_buf,
    nethot,
    quad,
    lhs_b,
    lhs_f,
    back,
    front,
    send_star,
    recv_star,
    send_cut,
    recv_cut,
    send2,
    recv2,
    dot_send,
    dot_recv,
    star_energy,
    vec_send,
    vec_recv,
    spr_send,
    spr_recv,
    sems,
    in_sems,
):
    count = regions * halves
    first_owner = regions // 4
    owner_regions = regions - 2 * first_owner
    owners = owner_regions * halves
    share = count // owners
    tiles = anchor_ref.shape[0]
    cut_groups = count // GROUP
    pin_chunks = pin_cell_ref.shape[0]
    pin_groups = pin_chunks // GROUP
    per_chunk = count // pin_chunks
    wide = GROUP * LANES
    my_region = lax.axis_index("region")
    my_half = lax.axis_index("coord")
    me = my_region * halves + my_half
    partner = (my_region, 1 - my_half)
    owning = jnp.logical_and(my_region >= first_owner, my_region < first_owner + owner_regions)
    my_share = (my_region - first_owner) * halves + my_half

    side = regions // 2
    my_side = my_region // side
    my_low = lax.rem(my_region, side)
    far_count = side * halves
    near_first = my_side * far_count
    far_start = (1 - my_side) * far_count

    def each_in(act, first_region, first_step):
        @pl.loop(first_step, side, unroll=True if regions <= 16 else 4)
        def _(step):
            low = my_low + step
            region = first_region + jnp.where(low >= side, low - side, low)
            for flip in range(halves):
                half = my_half if flip == 0 else 1 - my_half
                act(region * halves + half, (region, half))

    def each_far(act):
        each_in(act, (1 - my_side) * side, 0)

    def each_near(act):
        each_in(act, my_side * side, 1)
        act(my_region * halves + 1 - my_half, partner)

    def each_other(act):
        each_far(act)
        each_near(act)

    half_owners = owner_regions // 2
    regions_per_group = owner_regions // pin_groups
    farthest = half_owners - 1 - lax.rem(my_region, half_owners)
    farthest = farthest + jnp.where(my_region < regions // 2, half_owners, 0)
    farthest = farthest // regions_per_group

    def far_first(step):
        group = 0
        bit = 1
        while bit < pin_groups:
            group = group + lax.rem(farthest // bit + step // bit, 2) * bit
            bit *= 2
        return group

    def over_groups(groups, body):
        if groups <= 8:
            for group in range(groups):
                body(group)
        else:
            pl.loop(0, groups, unroll=4)(body)

    def sum_groups(groups, body, total):
        if groups <= 8:
            for group in range(groups):
                total = body(group, total)
            return total
        return lax.fori_loop(0, groups, body, total, unroll=4)

    barrier = pltpu.get_barrier_semaphore()

    def greet(other, device):
        pl.semaphore_signal(barrier, inc=1, device_id=device, device_id_type=MESH)

    each_other(greet)
    load = {}
    for k, (name, source, target) in enumerate(
        (
            ("pin_cell", pin_cell_hbm, pin_cell_ref),
            ("pin_net", pin_net_hbm, pin_net_ref),
            ("rs", rs_hbm, rs_ref),
            ("cut_cell", cut_cell_hbm, cut_cell_ref),
            ("nbr", nbr_row_hbm, nbr_row_ref),
            ("star_w", star_w_hbm, star_w_ref),
            ("cut_w", cut_w_hbm, cut_w_ref),
            ("anchor", anchor_hbm, anchor_ref),
            ("blocks", blocks_ref, block_buf),
        )
    ):
        load[name] = pltpu.make_async_copy(source, target, in_sems.at[k])
        load[name].start()
    star_energy[...] = jnp.zeros_like(star_energy)

    iota_lo = lax.broadcasted_iota(jnp.int32, (LANES, LANES), 0)
    iota_hi = lax.broadcasted_iota(jnp.int32, (tiles, LANES), 0)
    iota_net = lax.broadcasted_iota(jnp.int32, (per_chunk * LANES, LANES), 0)
    lane = lax.broadcasted_iota(jnp.int32, (1, LANES), 1)

    def put_onehot(group, place, cells):
        lanes = slice(place * LANES, (place + 1) * LANES)
        low = lax.bitwise_and(cells, LANES - 1)
        high = lax.shift_right_logical(cells, 7)
        onehot[group, :, lanes] = (iota_lo == low).astype(F32).astype(BF16)
        himask[group, :, lanes] = (iota_hi == high).astype(F32)

    def hot_pins(group):
        for place in range(GROUP):
            chunk = group * GROUP + place
            put_onehot(cut_groups + group, place, pin_cell_ref[pl.ds(chunk, 1), :])
            net = pin_net_ref[pl.ds(chunk, 1), :] - chunk * (per_chunk * LANES)
            nethot[chunk] = (iota_net == net).astype(F32).astype(BF16)

    def hot_cut(group):
        for place in range(GROUP):
            put_onehot(group, place, cut_cell_ref[pl.ds(group * GROUP + place, 1), :])

    load["pin_cell"].wait()
    load["pin_net"].wait()
    over_groups(pin_groups, hot_pins)

    def hold_blocks():
        load["blocks"].wait()

        @pl.loop(0, tiles, unroll=4)
        def _(tile):
            for k in range(2):
                high, low = pieces(block_buf[2 * tile + k])
                lanes = slice(k * LANES, (k + 1) * LANES)
                quad[tile, :LANES, lanes] = high
                quad[tile, LANES:, lanes] = low

        ones_row = jnp.where(lax.broadcasted_iota(jnp.int32, (8, 2 * LANES), 0) == 4, 1.0, 0.0)
        for tile in range(tiles):
            lhs_b[tile] = ones_row
            lhs_f[tile] = ones_row

    load["nbr"].wait()
    shift = my_half * tiles
    span = 2 * tiles
    rel_row = nbr_row_ref[...] - shift
    rel_row = jnp.where(rel_row < 0, rel_row + span, rel_row)
    on_diagonal = lax.broadcasted_iota(jnp.int32, (tiles, tiles), 0) == lax.broadcasted_iota(
        jnp.int32, (tiles, tiles), 1
    )
    rel_col = [
        jnp.sum(
            jnp.where(on_diagonal, rel_row[k : k + 1, :].astype(F32), 0.0), axis=1, keepdims=True
        ).astype(jnp.int32)
        for k in range(2)
    ]
    spread_hot = [
        (lax.broadcasted_iota(jnp.int32, (span, tiles), 0) == rel_row[k : k + 1, :])
        .astype(F32)
        .astype(BF16)
        for k in range(2)
    ]
    select_hot = [
        (lax.broadcasted_iota(jnp.int32, (tiles, span), 1) == rel_col[k])
        .astype(F32)
        .astype(BF16)
        for k in range(2)
    ]

    def rows8(first, second):
        fh, fl = pieces(first)
        sh, sl = pieces(second)
        stacked = jnp.concatenate(
            [x.astype(F32) for x in (fh, sh, fl, sl)]
            + [jnp.zeros((4, first.shape[1]), F32)],
            axis=0,
        )
        return stacked.astype(BF16)

    sub = lax.broadcasted_iota(jnp.int32, (8, wide), 0)
    in_half = sub < 4
    in_pair = lax.rem(sub, 4) < 2

    def fold_tiles(rows, mask):
        rows = rows * mask
        total = rows[:8]
        for t in range(8, tiles, 8):
            total = total + rows[t : t + 8]
        return total

    def fold_two(a, b):
        return jnp.where(in_half, a, b) + pltpu.roll(jnp.where(in_half, b, a), 4, 0)

    def gathered(group, left):
        got = mm(left, onehot[group])
        got = got[: 2 * tiles] + got[2 * tiles :]
        mask = himask[group]
        both = fold_two(fold_tiles(got[:tiles], mask), fold_tiles(got[tiles:], mask))
        both = both + pltpu.roll(both, 6, 0)
        both = both + pltpu.roll(both, 7, 0)
        return both[0:1], both[4:5]

    def gathered_pieces(group, left):
        got = mm(left, onehot[group])
        mask = himask[group]
        part = [fold_tiles(got[k * tiles : (k + 1) * tiles], mask) for k in range(4)]
        high = fold_two(part[0], part[1])
        low = fold_two(part[2], part[3])
        both = jnp.where(in_pair, high + pltpu.roll(high, 6, 0), low + pltpu.roll(low, 2, 0))
        return (both + pltpu.roll(both, 7, 0)).astype(BF16)

    def scattered(group, rows):
        mask = himask[group]
        spread = jnp.concatenate([mask * row for row in rows], axis=0)
        high, low = pieces(spread)
        both = mm(jnp.concatenate([high, low], axis=0), onehot[group], NT)
        rows_all = len(rows) * tiles
        return both[:rows_all] + both[rows_all:]

    def dot_rows(values):
        row = jnp.zeros((1, LANES), F32)
        for k, (a, b) in enumerate(values):
            total = jnp.sum(jnp.sum(a * b, axis=0, keepdims=True), axis=1, keepdims=True)
            row = jnp.where(lane == k, total, row)
        return row

    def halves_of(x):
        return x[:tiles], x[tiles:]

    def send_all(each, source_of, target, sent, arrived):
        def send(other, device):
            pltpu.make_async_remote_copy(
                src_ref=source_of(other),
                dst_ref=target.at[me],
                send_sem=sems.at[sent],
                recv_sem=sems.at[arrived],
                device_id=device,
                device_id_type=MESH,
            ).start()

        each(send)

    def wait_all(like, slot, messages=count - 1):
        part = like.at[pl.ds(0, messages)]
        pltpu.make_async_copy(part, part, sems.at[slot]).wait()

    def for_owner(act):
        pl.when(owning)(lambda: act(owners - 1))
        pl.when(jnp.logical_not(owning))(lambda: act(owners))

    def to_partner(source, target, slot):
        copy = pltpu.make_async_remote_copy(
            src_ref=source,
            dst_ref=target,
            send_sem=sems.at[slot],
            recv_sem=sems.at[slot + 1],
            device_id=partner,
            device_id_type=MESH,
        )
        copy.start()
        return copy

    def operate(turn, vector, dots, degree=None):
        first = turn == 0
        last = turn == ITERS - 1
        terms = 3 if first else 2
        base = turn * 14
        vec_send[turn] = vector
        if not first:
            vec_copy = to_partner(vec_send.at[turn], vec_recv.at[turn], base)
        high, low = pieces(vector)
        left = jnp.concatenate([high, low], axis=0)

        def star_values(group):
            rows = gathered_pieces(cut_groups + group, left)
            for place in range(GROUP):
                chunk = group * GROUP + place
                sums = mm(rows[:, place * LANES : (place + 1) * LANES], nethot[chunk], NT)
                sums = sums + pltpu.roll(sums, 6, 0)
                for r in range(per_chunk):
                    lanes = slice(r * LANES, (r + 1) * LANES)
                    for c in range(2):
                        send_star[turn, chunk * per_chunk + r, c : c + 1] = sums[
                            4 * c : 4 * c + 1, lanes
                        ]

        def to_owner(owner, device):
            pltpu.make_async_remote_copy(
                src_ref=send_star.at[turn, pl.ds(owner * share, share)],
                dst_ref=recv_star.at[turn, me],
                send_sem=sems.at[base + 2],
                recv_sem=sems.at[base + 3],
                device_id=device,
                device_id_type=MESH,
            ).start()

        def to_owners_of(group, nearest):
            for k in range(regions_per_group):
                place = group * regions_per_group + k
                act = functools.partial(to_owner, place * halves + my_half)
                device = (place + first_owner, my_half)
                to_owner(place * halves + 1 - my_half, (place + first_owner, 1 - my_half))
                if nearest:
                    pl.when(place + first_owner != my_region)(functools.partial(act, device))
                else:
                    act(device)

        over_groups(pin_groups, star_values)
        if first:
            pl.semaphore_wait(barrier, count - 1)
        for step in range(pin_groups):
            to_owners_of(far_first(step), step + 1 == pin_groups)

        @pl.when(owning)
        def _():
            recv_star[turn, me] = send_star[turn, pl.ds(my_share * share, share)]

        if first:
            vec_copy = to_partner(vec_send.at[turn], vec_recv.at[turn], base)
            load["cut_cell"].wait()
            over_groups(cut_groups, hot_cut)

        def cut_values(group):
            rows = gathered(group, left)
            for place in range(GROUP):
                lanes = slice(place * LANES, (place + 1) * LANES)
                send_cut[turn, group * GROUP + place] = jnp.concatenate(
                    [rows[0][:, lanes], rows[1][:, lanes]], axis=0
                )

        over_groups(cut_groups, cut_values)
        send_all(each_far, lambda o: send_cut.at[turn, o], recv_cut.at[turn], base + 8, base + 12)
        send_all(each_near, lambda o: send_cut.at[turn, o], recv_cut.at[turn], base + 8, base + 9)
        recv_cut[turn, me] = send_cut[turn, me]

        if first:
            hold_blocks()
        parts = (*halves_of(high.astype(F32)), *halves_of(low.astype(F32)))
        for r, part in enumerate(parts):
            lhs_b[:, r, :LANES] = part
            lhs_b[:, r, LANES:] = part
        for tile in range(tiles):
            out = mm(lhs_b[tile].astype(BF16), quad[tile])
            pair = out[0:2] + out[2:4]
            for k in range(2):
                lanes = slice(k * LANES, (k + 1) * LANES)
                for c in range(2):
                    back[k, tile : tile + 1, c * LANES : (c + 1) * LANES] = pair[
                        c : c + 1, lanes
                    ]
                if first:
                    back[k, tile : tile + 1, 2 * LANES :] = out[4:5, lanes]
        cols = terms * LANES
        spread = jnp.zeros((span, cols), F32)
        for k in range(2):
            bh, bl = pieces(back[k, :, :cols])
            spread = spread + mm(spread_hot[k], bh) + mm(spread_hot[k], bl)
        local = [spread[:tiles, c * LANES : (c + 1) * LANES] for c in range(terms)]
        for c in range(terms):
            spr_send[turn, c * tiles : (c + 1) * tiles] = spread[
                tiles:, c * LANES : (c + 1) * LANES
            ]
        if not first:
            spr_send[turn, 2 * tiles :] = jnp.zeros((tiles, LANES), F32)
        spr_copy = to_partner(spr_send.at[turn], spr_recv.at[turn], base + 4)

        vec_copy.wait()
        other = vec_recv[turn]
        whole = [
            jnp.concatenate([vector[c * tiles : (c + 1) * tiles], other[c * tiles : (c + 1) * tiles]], axis=0)
            for c in range(2)
        ]
        wh = [pieces(x) for x in whole]
        table = jnp.concatenate([wh[0][0], wh[1][0], wh[0][1], wh[1][1]], axis=1)
        for k in range(2):
            chosen = mm(select_hot[k], table)
            for r in range(4):
                lhs_f[:, r, k * LANES : (k + 1) * LANES] = chosen[:, r * LANES : (r + 1) * LANES]
        for tile in range(tiles):
            out = mm(lhs_f[tile].astype(BF16), quad[tile], NT)
            out = out[:, :LANES] + out[:, LANES:]
            pair = out[0:2] + out[2:4]
            for c in range(2):
                front[c, tile : tile + 1, :] = pair[c : c + 1]
            if first:
                front[2, tile : tile + 1, :] = out[4:5]
        local = [local[c] + front[c] for c in range(terms)]

        if first:
            load["star_w"].wait()

        @pl.when(owning)
        def _():
            wait_all(recv_star.at[turn], base + 3)
            totals = jnp.sum(recv_star[turn], axis=0)
            weight = star_w_ref[pl.ds(my_share * share, share), :] * (1.0 / FANOUT)
            weighted = totals * weight[:, None, :]
            send2[turn] = weighted

            def send(other, device):
                pltpu.make_async_remote_copy(
                    src_ref=send2.at[turn],
                    dst_ref=recv2.at[turn, pl.ds(my_share * share, share)],
                    send_sem=sems.at[base + 6],
                    recv_sem=sems.at[base + 7],
                    device_id=device,
                    device_id_type=MESH,
                ).start()

            each_other(send)
            recv2[turn, pl.ds(my_share * share, share)] = weighted
            if last:
                star_energy[...] = jnp.sum(weighted * totals, axis=0)

        if first:
            load["cut_w"].wait()
            load["anchor"].wait()
        else:
            dots = dots()
        wait_all(recv_cut.at[turn], base + 9, far_count - 1)
        if last:

            def across(start):
                part = pl.ds(start, far_count)
                terms_of = send_cut[turn, part] * recv_cut[turn, part] * cut_w_ref[part, :][:, None, :]
                return jnp.sum(terms_of, axis=0)

            near = across(near_first) + star_energy[...]
            energy = []
            for c in range(2):
                own = vector[c * tiles : (c + 1) * tiles]
                inner = own * (degree[:tiles] * own - 2.0 * front[c])
                rows = jnp.sum(inner, axis=0, keepdims=True) - near[c : c + 1]
                energy.append(jnp.sum(rows, axis=1, keepdims=True))
            for c in range(2):
                dots = jnp.where(lane == 18 + c, energy[c], dots)
        if not first:
            dot_send[turn, 0] = dots
            send_all(each_far, lambda o: dot_send.at[turn, 0], dot_recv.at[turn], base + 10, base + 11)
        wait_all(recv_cut.at[turn], base + 12, far_count)
        if last:
            far = 2.0 * across(far_start)
            for c in range(2):
                less = jnp.sum(far[c : c + 1], axis=1, keepdims=True)
                dots = jnp.where(lane == 18 + c, energy[c] - less, dots)
        if not first:
            dot_send[turn, 1] = dots
            send_all(each_near, lambda o: dot_send.at[turn, 1], dot_recv.at[turn], base + 10, base + 11)
            dot_recv[turn, me] = dots

        def cut_group(group, carry):
            weights = [cut_w_ref[pl.ds(group * GROUP + p, 1), :] for p in range(GROUP)]
            weight = jnp.concatenate(weights, axis=1)
            rows = [
                jnp.concatenate(
                    [recv_cut[turn, group * GROUP + p, c : c + 1, :] for p in range(GROUP)], axis=1
                )
                * weight
                for c in range(2)
            ]
            if first:
                rows.append(weight)
            return carry + scattered(group, rows)

        total = sum_groups(cut_groups, cut_group, jnp.zeros((terms * tiles, LANES), F32))

        def pin_weights(group, carry):
            row = []
            for place in range(GROUP):
                chunk = group * GROUP + place
                parts = [chunk * per_chunk + r for r in range(per_chunk)]
                own = jnp.concatenate([star_w_ref[pl.ds(o, 1), :] for o in parts], axis=1)
                got = mm(rows8(own, own), nethot[chunk])
                row.append(got[0:1] + got[2:3])
            return carry + scattered(cut_groups + group, [jnp.concatenate(row, axis=1)])

        if first:
            weighed = sum_groups(pin_groups, pin_weights, total[2 * tiles :])
        spr_copy.wait()
        for_owner(lambda n: wait_all(recv2.at[turn], base + 7, n * share))

        def pin_group(group, carry):
            rows = [[], []]
            for place in range(GROUP):
                chunk = group * GROUP + place
                parts = [chunk * per_chunk + r for r in range(per_chunk)]
                table = [
                    jnp.concatenate([recv2[turn, o, c : c + 1, :] for o in parts], axis=1)
                    for c in range(2)
                ]
                got = mm(rows8(*table), nethot[chunk])
                got = got[0:2] + got[2:4]
                for c in range(2):
                    rows[c].append(got[c : c + 1])
            return carry + scattered(
                cut_groups + group, [jnp.concatenate(r, axis=1) for r in rows]
            )

        total = sum_groups(pin_groups, pin_group, total[: 2 * tiles])
        if first:
            total = jnp.concatenate([total, weighed], axis=0)
        arrived = spr_recv[turn]
        both = jnp.concatenate(local, axis=0) + arrived[: terms * tiles] + total
        summed = None
        if not first:
            wait_all(dot_recv.at[turn], base + 11)
            summed = jnp.sum(dot_recv[turn], axis=0)
            wait_all(dot_recv.at[turn], base + 10)
        for_owner(lambda n: wait_all(send_star.at[turn], base + 2, n * share))
        wait_all(send_cut.at[turn], base + 8)

        @pl.when(owning)
        def _():
            wait_all(recv_star.at[turn], base + 6)

        return both, summed

    def pick(row, k):
        return jnp.sum(jnp.where(lane == k, row, 0.0), axis=1, keepdims=True)

    def stretch(pair):
        return jnp.concatenate(
            [jnp.broadcast_to(x, (tiles, LANES)) for x in pair], axis=0
        )

    def dots_of(pairs):
        return dot_rows([both for a, b in pairs for both in zip(halves_of(a), halves_of(b))])

    load["rs"].wait()
    r = jnp.concatenate(
        [
            rs_ref[c : c + 1, t * LANES : (t + 1) * LANES]
            for c in range(2)
            for t in range(tiles)
        ],
        axis=0,
    )
    both, _ = operate(0, r, None)
    degree = anchor_ref[...] + both[2 * tiles :]
    degree = jnp.concatenate([degree, degree], axis=0)
    w = degree * r - both[: 2 * tiles]
    x = jnp.zeros_like(r)
    p = s = z = None
    old_gamma = old_alpha = old_beta = beta = None
    for iteration in range(ITERS):
        if iteration + 1 < ITERS:
            pairs = [(r, r), (w, r)]
            if iteration + 2 == ITERS:
                pairs += [(r, s), (w, w), (w, s), (s, s), (w, z), (z, r), (z, s)]
            both, summed = operate(iteration + 1, w, functools.partial(dots_of, pairs), degree)
            q = degree * w - both
            gamma = [pick(summed, c) for c in range(2)]
            delta = [pick(summed, 2 + c) for c in range(2)]
        else:
            gamma, delta = [], []
            for c in range(2):
                rr, wr, rs, ww, ws, ss, wz, zr, zs, wq = [
                    pick(summed, 2 * k + c) for k in range(10)
                ]
                a, b = old_alpha[c], old_beta[c]
                ws_part = ww + b * ws
                gamma.append(
                    rr - 2.0 * a * (wr + b * rs) + a * a * (ws_part + b * (ws + b * ss))
                )
                w_next = wr - a * ws_part
                q_next = ww - a * (wq + b * wz)
                z_next = zr - a * (wz + b * zs)
                delta.append(w_next - a * (q_next + b * z_next))
        if iteration == 0:
            alpha = [gamma[c] / delta[c] for c in range(2)]
            p, s = r, w
            if iteration + 1 < ITERS:
                z = q
        else:
            beta = [gamma[c] / old_gamma[c] for c in range(2)]
            alpha = [
                gamma[c] / (delta[c] - beta[c] * gamma[c] / old_alpha[c]) for c in range(2)
            ]
            spread_beta = stretch(beta)
            p = r + spread_beta * p
            s = w + spread_beta * s
            if iteration + 1 < ITERS:
                z = q + spread_beta * z
        step = stretch(alpha)
        x = x + step * p
        r = r - step * s
        if iteration + 1 < ITERS:
            w = w - step * z
        old_gamma, old_alpha, old_beta = gamma, alpha, beta
    for c in range(2):
        for t in range(tiles):
            row = c * tiles + t
            lanes = slice(t * LANES, (t + 1) * LANES)
            out_ref[c : c + 1, lanes] = x[row : row + 1]
            out_ref[2 + c : 3 + c, lanes] = r[row : row + 1]


def per_device(
    regions,
    halves,
    right_side,
    anchor,
    blocks,
    tile_nbr,
    cut_cells,
    cut_weight,
    pin_cell,
    pin_net,
    star_weight,
):
    count = regions * halves
    tiles = blocks.shape[0]
    near = blocks.shape[1]
    pin_chunks = pin_cell.shape[0] // LANES
    per_chunk = count // pin_chunks
    groups = count // GROUP + pin_chunks // GROUP
    wide = GROUP * LANES
    share = count // ((regions - 2 * (regions // 4)) * halves)
    vmem = pl.BlockSpec(memory_space=pltpu.VMEM)
    shape = jax.ShapeDtypeStruct((4, tiles * LANES), F32)
    joint = pl.pallas_call(
        functools.partial(kernel, regions, halves),
        out_shape=shape,
        in_specs=[pl.BlockSpec(memory_space=pltpu.HBM)] * 9,
        out_specs=vmem,
        scratch_shapes=[
            pltpu.VMEM(right_side.shape, F32),
            pltpu.VMEM((tiles, LANES), F32),
            pltpu.VMEM((near, tiles), jnp.int32),
            pltpu.VMEM((count, LANES), jnp.int32),
            pltpu.VMEM((count, LANES), F32),
            pltpu.VMEM((pin_chunks, LANES), jnp.int32),
            pltpu.VMEM((pin_chunks, LANES), jnp.int32),
            pltpu.VMEM((count, LANES), F32),
            pltpu.VMEM((groups, LANES, wide), BF16),
            pltpu.VMEM((groups, tiles, wide), F32),
            pltpu.VMEM((tiles * near, LANES, LANES), F32),
            pltpu.VMEM((pin_chunks, per_chunk * LANES, LANES), BF16),
            pltpu.VMEM((tiles, 2 * LANES, 2 * LANES), BF16),
            pltpu.VMEM((tiles, 8, 2 * LANES), F32),
            pltpu.VMEM((tiles, 8, 2 * LANES), F32),
            pltpu.VMEM((2, tiles, 3 * LANES), F32),
            pltpu.VMEM((3, tiles, LANES), F32),
            pltpu.VMEM((ITERS, count, 2, LANES), F32),
            pltpu.VMEM((ITERS, count, share, 2, LANES), F32),
            pltpu.VMEM((ITERS, count, 2, LANES), F32),
            pltpu.VMEM((ITERS, count, 2, LANES), F32),
            pltpu.VMEM((ITERS, share, 2, LANES), F32),
            pltpu.VMEM((ITERS, count, 2, LANES), F32),
            pltpu.VMEM((ITERS, 2, 1, LANES), F32),
            pltpu.VMEM((ITERS, count, 1, LANES), F32),
            pltpu.VMEM((2, LANES), F32),
            pltpu.VMEM((ITERS, 2 * tiles, LANES), F32),
            pltpu.VMEM((ITERS, 2 * tiles, LANES), F32),
            pltpu.VMEM((ITERS, 3 * tiles, LANES), F32),
            pltpu.VMEM((ITERS, 3 * tiles, LANES), F32),
            pltpu.SemaphoreType.DMA((14 * ITERS,)),
            pltpu.SemaphoreType.DMA((9,)),
        ],
        compiler_params=pltpu.CompilerParams(
            collective_id=0, has_side_effects=True, vmem_limit_bytes=24 * 1024 * 1024
        ),
    )(*[pltpu.with_memory_space_constraint(v, pltpu.HBM) for v in (
        right_side,
        anchor.reshape(tiles, LANES),
        blocks.reshape(tiles * near, LANES, LANES),
        tile_nbr.T,
        cut_cells[0],
        cut_weight[0],
        pin_cell.reshape(pin_chunks, LANES),
        pin_net.reshape(pin_chunks, LANES),
        star_weight.reshape(count, LANES),
    )])
    return joint[:2], joint[2:]


def solution(mesh):
    return jax.shard_map(
        functools.partial(per_device, mesh.shape["region"], mesh.shape["coord"]),
        mesh=mesh,
        in_specs=(
            P(None, ("region", "coord")),
            P(("region", "coord")),
            P(("region", "coord"), None, None, None),
            P(("region", "coord"), None),
            P(("region", "coord"), None, None),
            P(("region", "coord"), None, None),
            P(("region", "coord")),
            P(("region", "coord")),
            P(),
        ),
        out_specs=(P(None, ("region", "coord")), P(None, ("region", "coord"))),
        check_vma=False,
    )
```

```python
import functools

import jax
import jax.numpy as jnp
from jax import lax
from jax.experimental import pallas as pl
from jax.experimental.pallas import tpu as pltpu
from jax.sharding import PartitionSpec as P

FANOUT = 32
ITERS = 3
LANES = 128
GROUP = 4
MESH = pl.DeviceIdType.MESH
F32 = jnp.float32
BF16 = jnp.bfloat16

NN = (((1,), (0,)), ((), ()))
NT = (((1,), (1,)), ((), ()))


def mm(a, b, dims=NN):
    return lax.dot_general(a, b, dims, preferred_element_type=F32)


def pieces(x):
    high = x.astype(BF16)
    low = (x - high.astype(F32)).astype(BF16)
    return high, low


def kernel(
    regions,
    halves,
    rs_hbm,
    anchor_hbm,
    blocks_ref,
    nbr_row_hbm,
    cut_cell_hbm,
    cut_w_hbm,
    pin_cell_hbm,
    pin_net_hbm,
    star_w_hbm,
    out_ref,
    rs_ref,
    anchor_ref,
    nbr_row_ref,
    cut_cell_ref,
    cut_w_ref,
    pin_cell_ref,
    pin_net_ref,
    star_w_ref,
    onehot,
    himask,
    block_buf,
    nethot,
    pinhot,
    quad,
    lhs_b,
    lhs_f,
    back,
    front,
    send_star,
    recv_star,
    send_cut,
    recv_cut,
    send2,
    recv2,
    dot_send,
    dot_recv,
    star_energy,
    vec_send,
    vec_recv,
    spr_send,
    spr_recv,
    sems,
    in_sems,
):
    count = regions * halves
    first_owner = regions // 4
    owner_regions = regions - 2 * first_owner
    owners = owner_regions * halves
    share = count // owners
    tiles = anchor_ref.shape[0]
    cut_groups = count // GROUP
    pin_chunks = pin_cell_ref.shape[0]
    pin_groups = pin_chunks // GROUP
    per_chunk = count // pin_chunks
    wide = GROUP * LANES
    my_region = lax.axis_index("region")
    my_half = lax.axis_index("coord")
    me = my_region * halves + my_half
    partner = (my_region, 1 - my_half)
    owning = jnp.logical_and(my_region >= first_owner, my_region < first_owner + owner_regions)
    my_share = (my_region - first_owner) * halves + my_half

    side = regions // 2
    my_side = my_region // side
    my_low = lax.rem(my_region, side)
    far_count = side * halves
    near_first = my_side * far_count
    far_start = (1 - my_side) * far_count

    def each_in(act, first_region, first_step):
        @pl.loop(first_step, side, unroll=True if regions <= 16 else 4)
        def _(step):
            low = my_low + step
            region = first_region + jnp.where(low >= side, low - side, low)
            for flip in range(halves):
                half = my_half if flip == 0 else 1 - my_half
                act(region * halves + half, (region, half))

    def each_far(act):
        each_in(act, (1 - my_side) * side, 0)

    def each_near(act):
        each_in(act, my_side * side, 1)
        act(my_region * halves + 1 - my_half, partner)

    def each_other(act):
        each_far(act)
        each_near(act)

    half_owners = owner_regions // 2
    regions_per_group = owner_regions // pin_groups
    farthest = half_owners - 1 - lax.rem(my_region, half_owners)
    farthest = farthest + jnp.where(my_region < regions // 2, half_owners, 0)
    farthest = farthest // regions_per_group

    def far_first(step):
        group = 0
        bit = 1
        while bit < pin_groups:
            group = group + lax.rem(farthest // bit + step // bit, 2) * bit
            bit *= 2
        return group

    def over_groups(groups, body):
        if groups <= 8:
            for group in range(groups):
                body(group)
        else:
            pl.loop(0, groups, unroll=4)(body)

    def sum_groups(groups, body, total):
        if groups <= 8:
            for group in range(groups):
                total = body(group, total)
            return total
        return lax.fori_loop(0, groups, body, total, unroll=4)

    barrier = pltpu.get_barrier_semaphore()

    def greet(other, device):
        pl.semaphore_signal(barrier, inc=1, device_id=device, device_id_type=MESH)

    each_other(greet)
    load = {}
    for k, (name, source, target) in enumerate(
        (
            ("pin_cell", pin_cell_hbm, pin_cell_ref),
            ("pin_net", pin_net_hbm, pin_net_ref),
            ("rs", rs_hbm, rs_ref),
            ("cut_cell", cut_cell_hbm, cut_cell_ref),
            ("nbr", nbr_row_hbm, nbr_row_ref),
            ("star_w", star_w_hbm, star_w_ref),
            ("cut_w", cut_w_hbm, cut_w_ref),
            ("anchor", anchor_hbm, anchor_ref),
            ("blocks", blocks_ref, block_buf),
        )
    ):
        load[name] = pltpu.make_async_copy(source, target, in_sems.at[k])
        load[name].start()
    star_energy[...] = jnp.zeros_like(star_energy)

    iota_lo = lax.broadcasted_iota(jnp.int32, (LANES, LANES), 0)
    iota_hi = lax.broadcasted_iota(jnp.int32, (tiles, LANES), 0)
    iota_net = lax.broadcasted_iota(jnp.int32, (per_chunk * LANES, LANES), 0)
    lane = lax.broadcasted_iota(jnp.int32, (1, LANES), 1)

    def put_onehot(group, place, cells):
        lanes = slice(place * LANES, (place + 1) * LANES)
        low = lax.bitwise_and(cells, LANES - 1)
        high = lax.shift_right_logical(cells, 7)
        onehot[group, :, lanes] = (iota_lo == low).astype(F32).astype(BF16)
        himask[group, :, lanes] = (iota_hi == high).astype(F32)

    def hot_pins(group):
        for place in range(GROUP):
            chunk = group * GROUP + place
            put_onehot(cut_groups + group, place, pin_cell_ref[pl.ds(chunk, 1), :])
            net = pin_net_ref[pl.ds(chunk, 1), :] - chunk * (per_chunk * LANES)
            nethot[chunk] = (iota_net == net).astype(F32).astype(BF16)

    def hot_cut(group):
        for place in range(GROUP):
            put_onehot(group, place, cut_cell_ref[pl.ds(group * GROUP + place, 1), :])

    load["pin_cell"].wait()
    load["pin_net"].wait()
    over_groups(pin_groups, hot_pins)

    def hold_blocks():
        load["blocks"].wait()

        @pl.loop(0, tiles, unroll=4)
        def _(tile):
            for k in range(2):
                high, low = pieces(block_buf[2 * tile + k])
                lanes = slice(k * LANES, (k + 1) * LANES)
                quad[tile, :LANES, lanes] = high
                quad[tile, LANES:, lanes] = low

        ones_row = jnp.where(lax.broadcasted_iota(jnp.int32, (8, 2 * LANES), 0) == 4, 1.0, 0.0)
        for tile in range(tiles):
            lhs_b[tile] = ones_row
            lhs_f[tile] = ones_row

    load["nbr"].wait()
    shift = my_half * tiles
    span = 2 * tiles
    rel_row = nbr_row_ref[...] - shift
    rel_row = jnp.where(rel_row < 0, rel_row + span, rel_row)
    on_diagonal = lax.broadcasted_iota(jnp.int32, (tiles, tiles), 0) == lax.broadcasted_iota(
        jnp.int32, (tiles, tiles), 1
    )
    rel_col = [
        jnp.sum(
            jnp.where(on_diagonal, rel_row[k : k + 1, :].astype(F32), 0.0), axis=1, keepdims=True
        ).astype(jnp.int32)
        for k in range(2)
    ]
    spread_hot = [
        (lax.broadcasted_iota(jnp.int32, (span, tiles), 0) == rel_row[k : k + 1, :])
        .astype(F32)
        .astype(BF16)
        for k in range(2)
    ]
    select_hot = [
        (lax.broadcasted_iota(jnp.int32, (tiles, span), 1) == rel_col[k])
        .astype(F32)
        .astype(BF16)
        for k in range(2)
    ]

    def rows8(first, second):
        fh, fl = pieces(first)
        sh, sl = pieces(second)
        stacked = jnp.concatenate(
            [x.astype(F32) for x in (fh, sh, fl, sl)]
            + [jnp.zeros((4, first.shape[1]), F32)],
            axis=0,
        )
        return stacked.astype(BF16)

    sub = lax.broadcasted_iota(jnp.int32, (8, wide), 0)
    in_half = sub < 4
    in_pair = lax.rem(sub, 4) < 2

    def fold_tiles(rows, mask):
        rows = rows * mask
        total = rows[:8]
        for t in range(8, tiles, 8):
            total = total + rows[t : t + 8]
        return total

    def fold_two(a, b):
        return jnp.where(in_half, a, b) + pltpu.roll(jnp.where(in_half, b, a), 4, 0)

    def gathered(group, left):
        got = mm(left, onehot[group])
        got = got[: 2 * tiles] + got[2 * tiles :]
        mask = himask[group]
        both = fold_two(fold_tiles(got[:tiles], mask), fold_tiles(got[tiles:], mask))
        both = both + pltpu.roll(both, 6, 0)
        both = both + pltpu.roll(both, 7, 0)
        return both[0:1], both[4:5]

    def gathered_pieces(group, left):
        got = mm(left, onehot[group])
        mask = himask[group]
        part = [fold_tiles(got[k * tiles : (k + 1) * tiles], mask) for k in range(4)]
        high = fold_two(part[0], part[1])
        low = fold_two(part[2], part[3])
        both = jnp.where(in_pair, high + pltpu.roll(high, 6, 0), low + pltpu.roll(low, 2, 0))
        return (both + pltpu.roll(both, 7, 0)).astype(BF16)

    def scattered(group, rows):
        mask = himask[group]
        spread = jnp.concatenate([mask * row for row in rows], axis=0)
        high, low = pieces(spread)
        both = mm(jnp.concatenate([high, low], axis=0), onehot[group], NT)
        rows_all = len(rows) * tiles
        return both[:rows_all] + both[rows_all:]

    def dot_rows(values):
        row = jnp.zeros((1, LANES), F32)
        for k, (a, b) in enumerate(values):
            total = jnp.sum(jnp.sum(a * b, axis=0, keepdims=True), axis=1, keepdims=True)
            row = jnp.where(lane == k, total, row)
        return row

    def halves_of(x):
        return x[:tiles], x[tiles:]

    def send_all(each, source_of, target, sent, arrived):
        def send(other, device):
            pltpu.make_async_remote_copy(
                src_ref=source_of(other),
                dst_ref=target.at[me],
                send_sem=sems.at[sent],
                recv_sem=sems.at[arrived],
                device_id=device,
                device_id_type=MESH,
            ).start()

        each(send)

    def wait_all(like, slot, messages=count - 1):
        part = like.at[pl.ds(0, messages)]
        pltpu.make_async_copy(part, part, sems.at[slot]).wait()

    def for_owner(act):
        pl.when(owning)(lambda: act(owners - 1))
        pl.when(jnp.logical_not(owning))(lambda: act(owners))

    def to_partner(source, target, slot):
        copy = pltpu.make_async_remote_copy(
            src_ref=source,
            dst_ref=target,
            send_sem=sems.at[slot],
            recv_sem=sems.at[slot + 1],
            device_id=partner,
            device_id_type=MESH,
        )
        copy.start()
        return copy

    def operate(turn, vector, dots, degree=None):
        first = turn == 0
        last = turn == ITERS - 1
        terms = 3 if first else 2
        base = turn * 14
        vec_send[turn] = vector
        if not first:
            vec_copy = to_partner(vec_send.at[turn], vec_recv.at[turn], base)
        high, low = pieces(vector)
        left = jnp.concatenate([high, low], axis=0)

        def star_rows(group):
            return gathered_pieces(cut_groups + group, left)

        def star_sums(group, rows):
            for place in range(GROUP):
                chunk = group * GROUP + place
                sums = mm(rows[:, place * LANES : (place + 1) * LANES], *((nethot[chunk], NT) if first else (pinhot[chunk], NN)))
                sums = sums + pltpu.roll(sums, 6, 0)
                for r in range(per_chunk):
                    lanes = slice(r * LANES, (r + 1) * LANES)
                    for c in range(2):
                        send_star[turn, chunk * per_chunk + r, c : c + 1] = sums[
                            4 * c : 4 * c + 1, lanes
                        ]

        def to_owner(owner, device):
            pltpu.make_async_remote_copy(
                src_ref=send_star.at[turn, pl.ds(owner * share, share)],
                dst_ref=recv_star.at[turn, me],
                send_sem=sems.at[base + 2],
                recv_sem=sems.at[base + 3],
                device_id=device,
                device_id_type=MESH,
            ).start()

        def to_owners_of(group, nearest):
            for k in range(regions_per_group):
                place = group * regions_per_group + k
                act = functools.partial(to_owner, place * halves + my_half)
                device = (place + first_owner, my_half)
                to_owner(place * halves + 1 - my_half, (place + first_owner, 1 - my_half))
                if nearest:
                    pl.when(place + first_owner != my_region)(functools.partial(act, device))
                else:
                    act(device)

        together = [star_rows(group) for group in range(pin_groups)]
        for group in range(pin_groups):
            star_sums(group, together[group])
        if first:
            pl.semaphore_wait(barrier, count - 1)
        for step in range(pin_groups):
            to_owners_of(far_first(step), step + 1 == pin_groups)

        @pl.when(owning)
        def _():
            recv_star[turn, me] = send_star[turn, pl.ds(my_share * share, share)]

        if first:
            vec_copy = to_partner(vec_send.at[turn], vec_recv.at[turn], base)
            load["cut_cell"].wait()
            over_groups(cut_groups, hot_cut)

        def cut_values(group):
            rows = gathered(group, left)
            for place in range(GROUP):
                lanes = slice(place * LANES, (place + 1) * LANES)
                send_cut[turn, group * GROUP + place] = jnp.concatenate(
                    [rows[0][:, lanes], rows[1][:, lanes]], axis=0
                )

        over_groups(cut_groups, cut_values)
        send_all(each_far, lambda o: send_cut.at[turn, o], recv_cut.at[turn], base + 8, base + 12)
        send_all(each_near, lambda o: send_cut.at[turn, o], recv_cut.at[turn], base + 8, base + 9)
        recv_cut[turn, me] = send_cut[turn, me]

        if first:

            @pl.loop(0, pin_chunks, unroll=8)
            def _(chunk):
                pinhot[chunk] = nethot[chunk].astype(F32).T.astype(BF16)

            hold_blocks()
        parts = (*halves_of(high.astype(F32)), *halves_of(low.astype(F32)))
        for r, part in enumerate(parts):
            lhs_b[:, r, :LANES] = part
            lhs_b[:, r, LANES:] = part
        for tile in range(tiles):
            out = mm(lhs_b[tile].astype(BF16), quad[tile])
            pair = out[0:2] + out[2:4]
            for k in range(2):
                lanes = slice(k * LANES, (k + 1) * LANES)
                for c in range(2):
                    back[k, tile : tile + 1, c * LANES : (c + 1) * LANES] = pair[
                        c : c + 1, lanes
                    ]
                if first:
                    back[k, tile : tile + 1, 2 * LANES :] = out[4:5, lanes]
        cols = terms * LANES
        spread = jnp.zeros((span, cols), F32)
        for k in range(2):
            bh, bl = pieces(back[k, :, :cols])
            spread = spread + mm(spread_hot[k], bh) + mm(spread_hot[k], bl)
        local = [spread[:tiles, c * LANES : (c + 1) * LANES] for c in range(terms)]
        for c in range(terms):
            spr_send[turn, c * tiles : (c + 1) * tiles] = spread[
                tiles:, c * LANES : (c + 1) * LANES
            ]
        if not first:
            spr_send[turn, 2 * tiles :] = jnp.zeros((tiles, LANES), F32)
        spr_copy = to_partner(spr_send.at[turn], spr_recv.at[turn], base + 4)

        vec_copy.wait()
        other = vec_recv[turn]
        whole = [
            jnp.concatenate([vector[c * tiles : (c + 1) * tiles], other[c * tiles : (c + 1) * tiles]], axis=0)
            for c in range(2)
        ]
        wh = [pieces(x) for x in whole]
        table = jnp.concatenate([wh[0][0], wh[1][0], wh[0][1], wh[1][1]], axis=1)
        for k in range(2):
            chosen = mm(select_hot[k], table)
            for r in range(4):
                lhs_f[:, r, k * LANES : (k + 1) * LANES] = chosen[:, r * LANES : (r + 1) * LANES]
        for tile in range(tiles):
            out = mm(lhs_f[tile].astype(BF16), quad[tile], NT)
            out = out[:, :LANES] + out[:, LANES:]
            pair = out[0:2] + out[2:4]
            for c in range(2):
                front[c, tile : tile + 1, :] = pair[c : c + 1]
            if first:
                front[2, tile : tile + 1, :] = out[4:5]
        local = [local[c] + front[c] for c in range(terms)]

        if first:
            load["star_w"].wait()

        @pl.when(owning)
        def _():
            wait_all(recv_star.at[turn], base + 3)
            totals = jnp.sum(recv_star[turn], axis=0)
            weight = star_w_ref[pl.ds(my_share * share, share), :] * (1.0 / FANOUT)
            weighted = totals * weight[:, None, :]
            send2[turn] = weighted

            def send(other, device):
                pltpu.make_async_remote_copy(
                    src_ref=send2.at[turn],
                    dst_ref=recv2.at[turn, pl.ds(my_share * share, share)],
                    send_sem=sems.at[base + 6],
                    recv_sem=sems.at[base + 7],
                    device_id=device,
                    device_id_type=MESH,
                ).start()

            each_other(send)
            recv2[turn, pl.ds(my_share * share, share)] = weighted
            if last:
                star_energy[...] = jnp.sum(weighted * totals, axis=0)

        if first:
            load["cut_w"].wait()
            load["anchor"].wait()
        else:
            dots = dots()
        wait_all(recv_cut.at[turn], base + 9, far_count - 1)
        if last:

            def across(start):
                part = pl.ds(start, far_count)
                terms_of = send_cut[turn, part] * recv_cut[turn, part] * cut_w_ref[part, :][:, None, :]
                return jnp.sum(terms_of, axis=0)

            near = across(near_first) + star_energy[...]
            energy = []
            for c in range(2):
                own = vector[c * tiles : (c + 1) * tiles]
                inner = own * (degree[:tiles] * own - 2.0 * front[c])
                rows = jnp.sum(inner, axis=0, keepdims=True) - near[c : c + 1]
                energy.append(jnp.sum(rows, axis=1, keepdims=True))
            for c in range(2):
                dots = jnp.where(lane == 18 + c, energy[c], dots)
        if not first:
            dot_send[turn, 0] = dots
            send_all(each_far, lambda o: dot_send.at[turn, 0], dot_recv.at[turn], base + 10, base + 11)
        wait_all(recv_cut.at[turn], base + 12, far_count)
        if last:
            far = 2.0 * across(far_start)
            for c in range(2):
                less = jnp.sum(far[c : c + 1], axis=1, keepdims=True)
                dots = jnp.where(lane == 18 + c, energy[c] - less, dots)
        if not first:
            dot_send[turn, 1] = dots
            send_all(each_near, lambda o: dot_send.at[turn, 1], dot_recv.at[turn], base + 10, base + 11)
            dot_recv[turn, me] = dots

        def cut_group(group, carry):
            weights = [cut_w_ref[pl.ds(group * GROUP + p, 1), :] for p in range(GROUP)]
            weight = jnp.concatenate(weights, axis=1)
            rows = [
                jnp.concatenate(
                    [recv_cut[turn, group * GROUP + p, c : c + 1, :] for p in range(GROUP)], axis=1
                )
                * weight
                for c in range(2)
            ]
            if first:
                rows.append(weight)
            return carry + scattered(group, rows)

        total = sum_groups(cut_groups, cut_group, jnp.zeros((terms * tiles, LANES), F32))

        def pin_weights(group, carry):
            row = []
            for place in range(GROUP):
                chunk = group * GROUP + place
                parts = [chunk * per_chunk + r for r in range(per_chunk)]
                own = jnp.concatenate([star_w_ref[pl.ds(o, 1), :] for o in parts], axis=1)
                got = mm(rows8(own, own), nethot[chunk])
                row.append(got[0:1] + got[2:3])
            return carry + scattered(cut_groups + group, [jnp.concatenate(row, axis=1)])

        if first:
            weighed = sum_groups(pin_groups, pin_weights, total[2 * tiles :])
        spr_copy.wait()
        for_owner(lambda n: wait_all(recv2.at[turn], base + 7, n * share))

        def pin_group(group, carry):
            rows = [[], []]
            for place in range(GROUP):
                chunk = group * GROUP + place
                parts = [chunk * per_chunk + r for r in range(per_chunk)]
                table = [
                    jnp.concatenate([recv2[turn, o, c : c + 1, :] for o in parts], axis=1)
                    for c in range(2)
                ]
                got = mm(rows8(*table), nethot[chunk])
                got = got[0:2] + got[2:4]
                for c in range(2):
                    rows[c].append(got[c : c + 1])
            return carry + scattered(
                cut_groups + group, [jnp.concatenate(r, axis=1) for r in rows]
            )

        total = sum_groups(pin_groups, pin_group, total[: 2 * tiles])
        if first:
            total = jnp.concatenate([total, weighed], axis=0)
        arrived = spr_recv[turn]
        both = jnp.concatenate(local, axis=0) + arrived[: terms * tiles] + total
        summed = None
        if not first:
            wait_all(dot_recv.at[turn], base + 11)
            summed = jnp.sum(dot_recv[turn], axis=0)
            wait_all(dot_recv.at[turn], base + 10)
        for_owner(lambda n: wait_all(send_star.at[turn], base + 2, n * share))
        wait_all(send_cut.at[turn], base + 8)

        @pl.when(owning)
        def _():
            wait_all(recv_star.at[turn], base + 6)

        return both, summed

    def pick(row, k):
        return jnp.sum(jnp.where(lane == k, row, 0.0), axis=1, keepdims=True)

    def stretch(pair):
        return jnp.concatenate(
            [jnp.broadcast_to(x, (tiles, LANES)) for x in pair], axis=0
        )

    def dots_of(pairs):
        return dot_rows([both for a, b in pairs for both in zip(halves_of(a), halves_of(b))])

    load["rs"].wait()
    r = jnp.concatenate(
        [
            rs_ref[c : c + 1, t * LANES : (t + 1) * LANES]
            for c in range(2)
            for t in range(tiles)
        ],
        axis=0,
    )
    both, _ = operate(0, r, None)
    degree = anchor_ref[...] + both[2 * tiles :]
    degree = jnp.concatenate([degree, degree], axis=0)
    w = degree * r - both[: 2 * tiles]
    x = jnp.zeros_like(r)
    p = s = z = None
    old_gamma = old_alpha = old_beta = beta = None
    for iteration in range(ITERS):
        if iteration + 1 < ITERS:
            pairs = [(r, r), (w, r)]
            if iteration + 2 == ITERS:
                pairs += [(r, s), (w, w), (w, s), (s, s), (w, z), (z, r), (z, s)]
            both, summed = operate(iteration + 1, w, functools.partial(dots_of, pairs), degree)
            q = degree * w - both
            gamma = [pick(summed, c) for c in range(2)]
            delta = [pick(summed, 2 + c) for c in range(2)]
        else:
            gamma, delta = [], []
            for c in range(2):
                rr, wr, rs, ww, ws, ss, wz, zr, zs, wq = [
                    pick(summed, 2 * k + c) for k in range(10)
                ]
                a, b = old_alpha[c], old_beta[c]
                ws_part = ww + b * ws
                gamma.append(
                    rr - 2.0 * a * (wr + b * rs) + a * a * (ws_part + b * (ws + b * ss))
                )
                w_next = wr - a * ws_part
                q_next = ww - a * (wq + b * wz)
                z_next = zr - a * (wz + b * zs)
                delta.append(w_next - a * (q_next + b * z_next))
        if iteration == 0:
            alpha = [gamma[c] / delta[c] for c in range(2)]
            p, s = r, w
            if iteration + 1 < ITERS:
                z = q
        else:
            beta = [gamma[c] / old_gamma[c] for c in range(2)]
            alpha = [
                gamma[c] / (delta[c] - beta[c] * gamma[c] / old_alpha[c]) for c in range(2)
            ]
            spread_beta = stretch(beta)
            p = r + spread_beta * p
            s = w + spread_beta * s
            if iteration + 1 < ITERS:
                z = q + spread_beta * z
        step = stretch(alpha)
        x = x + step * p
        r = r - step * s
        if iteration + 1 < ITERS:
            w = w - step * z
        old_gamma, old_alpha, old_beta = gamma, alpha, beta
    for c in range(2):
        for t in range(tiles):
            row = c * tiles + t
            lanes = slice(t * LANES, (t + 1) * LANES)
            out_ref[c : c + 1, lanes] = x[row : row + 1]
            out_ref[2 + c : 3 + c, lanes] = r[row : row + 1]


def per_device(
    regions,
    halves,
    right_side,
    anchor,
    blocks,
    tile_nbr,
    cut_cells,
    cut_weight,
    pin_cell,
    pin_net,
    star_weight,
):
    count = regions * halves
    tiles = blocks.shape[0]
    near = blocks.shape[1]
    pin_chunks = pin_cell.shape[0] // LANES
    per_chunk = count // pin_chunks
    groups = count // GROUP + pin_chunks // GROUP
    wide = GROUP * LANES
    share = count // ((regions - 2 * (regions // 4)) * halves)
    vmem = pl.BlockSpec(memory_space=pltpu.VMEM)
    shape = jax.ShapeDtypeStruct((4, tiles * LANES), F32)
    joint = pl.pallas_call(
        functools.partial(kernel, regions, halves),
        out_shape=shape,
        in_specs=[pl.BlockSpec(memory_space=pltpu.HBM)] * 9,
        out_specs=vmem,
        scratch_shapes=[
            pltpu.VMEM(right_side.shape, F32),
            pltpu.VMEM((tiles, LANES), F32),
            pltpu.VMEM((near, tiles), jnp.int32),
            pltpu.VMEM((count, LANES), jnp.int32),
            pltpu.VMEM((count, LANES), F32),
            pltpu.VMEM((pin_chunks, LANES), jnp.int32),
            pltpu.VMEM((pin_chunks, LANES), jnp.int32),
            pltpu.VMEM((count, LANES), F32),
            pltpu.VMEM((groups, LANES, wide), BF16),
            pltpu.VMEM((groups, tiles, wide), F32),
            pltpu.VMEM((tiles * near, LANES, LANES), F32),
            pltpu.VMEM((pin_chunks, per_chunk * LANES, LANES), BF16),
            pltpu.VMEM((pin_chunks, LANES, per_chunk * LANES), BF16),
            pltpu.VMEM((tiles, 2 * LANES, 2 * LANES), BF16),
            pltpu.VMEM((tiles, 8, 2 * LANES), F32),
            pltpu.VMEM((tiles, 8, 2 * LANES), F32),
            pltpu.VMEM((2, tiles, 3 * LANES), F32),
            pltpu.VMEM((3, tiles, LANES), F32),
            pltpu.VMEM((ITERS, count, 2, LANES), F32),
            pltpu.VMEM((ITERS, count, share, 2, LANES), F32),
            pltpu.VMEM((ITERS, count, 2, LANES), F32),
            pltpu.VMEM((ITERS, count, 2, LANES), F32),
            pltpu.VMEM((ITERS, share, 2, LANES), F32),
            pltpu.VMEM((ITERS, count, 2, LANES), F32),
            pltpu.VMEM((ITERS, 2, 1, LANES), F32),
            pltpu.VMEM((ITERS, count, 1, LANES), F32),
            pltpu.VMEM((2, LANES), F32),
            pltpu.VMEM((ITERS, 2 * tiles, LANES), F32),
            pltpu.VMEM((ITERS, 2 * tiles, LANES), F32),
            pltpu.VMEM((ITERS, 3 * tiles, LANES), F32),
            pltpu.VMEM((ITERS, 3 * tiles, LANES), F32),
            pltpu.SemaphoreType.DMA((14 * ITERS,)),
            pltpu.SemaphoreType.DMA((9,)),
        ],
        compiler_params=pltpu.CompilerParams(
            collective_id=0, has_side_effects=True, vmem_limit_bytes=24 * 1024 * 1024
        ),
    )(*[pltpu.with_memory_space_constraint(v, pltpu.HBM) for v in (
        right_side,
        anchor.reshape(tiles, LANES),
        blocks.reshape(tiles * near, LANES, LANES),
        tile_nbr.T,
        cut_cells[0],
        cut_weight[0],
        pin_cell.reshape(pin_chunks, LANES),
        pin_net.reshape(pin_chunks, LANES),
        star_weight.reshape(count, LANES),
    )])
    return joint[:2], joint[2:]


def solution(mesh):
    return jax.shard_map(
        functools.partial(per_device, mesh.shape["region"], mesh.shape["coord"]),
        mesh=mesh,
        in_specs=(
            P(None, ("region", "coord")),
            P(("region", "coord")),
            P(("region", "coord"), None, None, None),
            P(("region", "coord"), None),
            P(("region", "coord"), None, None),
            P(("region", "coord"), None, None),
            P(("region", "coord")),
            P(("region", "coord")),
            P(),
        ),
        out_specs=(P(None, ("region", "coord")), P(None, ("region", "coord"))),
        check_vma=False,
    )
```
